128 devices in a mesh: wide: 32 (over z_lo, y, x), narrow: 4 (over z_hi, core).
Axes of the slice: x: 4, y: 4, z: 4 (z_hi: 2, z_lo: 2; z = z_hi * 2 + z_lo), core: 2. Of those that a mesh axis runs over, the one named last changes fastest.
Arguments:
- activations: bfloat16 [1024, 28672], P('wide', 'narrow'), may hold values from -6 to 6
- out_grads: bfloat16 [1024, 8192], P('narrow', 'wide'), may hold values from -0.25976562 to 0.25976562
- basis_in: bfloat16 [28672, 28672], P('narrow', 'wide'), may hold values from -0.03125 to 0.03125
- basis_out: bfloat16 [8192, 8192], P('wide', 'narrow'), may hold values from -0.0625 to 0.0625
Outputs:
- corrections: float32 [8192, 28672], P('narrow', 'wide')
The draws below stay inside these ranges and needn't reach their ends.
All inputs are finite; a program needn't handle non-finite values.
Results may differ from the reference program's by a relative error of at most 0.0042.
Values may be sent and summed in bfloat16 or wider, within the bound.
A program may use at most 128 MiB of HBM per device.

```python
import jax
import jax.numpy as jnp
from jax import lax

DIN = 28672
DOUT = 8192
SEQ_LEN = 512
SEQS = 2
TOKENS = 1024


def steps_of(stream_key, shape, split, low, high):
    gain, own = 1.0, jax.random.fold_in(stream_key, 6)
    for position, shards_of in split:
        heights = jnp.exp(jax.random.uniform(jax.random.fold_in(own, position), (shards_of,), jnp.float32, low / len(split), high / len(split)))
        gain = gain * jnp.repeat(heights, shape[position] // shards_of).reshape([-1 if axis == position else 1 for axis in range(len(shape))])
    return gain


def gaussian(stream_key, dims, scale, reach, pieces=(), kind=jnp.bfloat16):
    loudness = steps_of(stream_key, dims, pieces, -0.22, 0.18) if pieces else 1.0
    entries = jax.random.normal(stream_key, dims, jnp.float32) * scale * loudness
    return jnp.minimum(jnp.maximum(entries, -reach), reach).astype(kind)


def setup_inputs(seed: int = 0) -> dict:
    streams_of = jax.random.split(jax.random.key(seed), 5)
    activations = gaussian(streams_of[0], (TOKENS, DIN), 1.0, 6.0, ((0, 32), (1, 4)))
    out_grads = gaussian(streams_of[1], (TOKENS, DOUT), 0.044, 0.25976562, ((0, 4), (1, 32)))
    basis_in = gaussian(streams_of[2], (DIN, DIN), DIN ** -0.5, 0.03125, ((0, 4), (1, 32)))
    basis_out = gaussian(streams_of[3], (DOUT, DOUT), DOUT ** -0.5, 0.0625, ((0, 32), (1, 4)))
    return {"activations": activations, "out_grads": out_grads, "basis_in": basis_in, "basis_out": basis_out}


def reference(activations, out_grads, basis_in, basis_out):
    rot_in = jnp.dot(activations, basis_in, preferred_element_type=jnp.float32).astype(jnp.bfloat16)
    rot_out = jnp.dot(out_grads, basis_out, preferred_element_type=jnp.float32).astype(jnp.bfloat16)
    rot_in = rot_in.reshape(SEQS, SEQ_LEN, DIN)
    rot_out = rot_out.reshape(SEQS, SEQ_LEN, DOUT)

    def accumulate(total, pair):
        grads_seq, inputs_seq = pair
        rotated = jnp.dot(grads_seq.T, inputs_seq, preferred_element_type=jnp.float32)
        return total + rotated * rotated, None

    start_total = jnp.zeros((DOUT, DIN), jnp.float32)
    total, unused = lax.scan(accumulate, start_total, (rot_out, rot_in))
    return total / SEQS
```

```python
import functools

import jax
import jax.numpy as jnp
from jax import lax
from jax.experimental import pallas as pl
from jax.experimental.pallas import tpu as pltpu
from jax.sharding import PartitionSpec as P

MESH = pl.DeviceIdType.MESH
BF, F32 = jnp.bfloat16, jnp.float32
SEQS = 2
ROWS = 32
HALF = 16
RING = 4
T = 128

RATE = 45000.0
LAT = 2.0

PIECES = (
    ((17, "zxy"), (17, "zyx"), (11, "xyz"), (11, "yxz")),
    ((17, "zxy"), (17, "zyx"), (11, "xyz"), (11, "yxz")),
)
OUT_GATHER = ("zxy", "zyx")
OUT_REDUCE = ("yxz", "xyz")


class Tasks:
    def __init__(self):
        self.items = []
        self.index = {}

    def add(self, name, deps, emit, kind, link=None, cost=0.0, prio=0.0):
        self.index[name] = len(self.items)
        self.items.append((name, tuple(deps), emit, kind, link, cost, prio))

    def order(self):
        start = {}
        ready_at = {}
        free = {}
        left = list(range(len(self.items)))
        now, result = 0.0, []
        while left:
            best, soonest = None, None
            for i in left:
                name, deps, _, kind, link, cost, prio = self.items[i]
                if any(d not in ready_at for d in deps):
                    continue
                at = max([ready_at[d] for d in deps], default=0.0)
                if at <= now:
                    key = (0 if kind == "send" else 1, prio, i)
                    if best is None or key < best[0]:
                        best = (key, i)
                elif soonest is None or at < soonest:
                    soonest = at
            if best is None:
                now = soonest
                continue
            i = best[1]
            name, deps, _, kind, link, cost, prio = self.items[i]
            left.remove(i)
            result.append(i)
            start[name] = now
            if kind == "send":
                begin = max(now, free.get(link, 0.0))
                free[link] = begin + cost
                ready_at[name] = begin + cost + LAT
                now += 0.02
            else:
                now += cost
                ready_at[name] = now
        return result, ready_at, start, free


def ax_index(axis, where, at, gathered):
    return slice(None) if axis in gathered else at.get(axis, where[axis])


def build(t, refs, where, make):
    (acts, grads, bin_, bout, ri_out, ro_out, abuf, bvm, part, qb, ro, rs, ex, ri, gvm, bovm, lsem) = refs
    x, y, z, zh, core = (where[k] for k in ("x", "y", "z", "zh", "core"))

    def nxt(axis, d):
        return lax.rem(where[axis] + (RING + d), RING)

    def gather(tag, buf, dtype_bytes, rows, col, width, order, deps, prio):
        gathered = ()
        blocks = 1
        for axis in order:
            def region(at, c, w, gathered=gathered, axis=axis):
                i = tuple(ax_index(a, where, {axis: at}, gathered) for a in "zyx")
                return buf.at[i + (slice(None), pl.ds(c, w))]
            bytes_ = blocks * rows * dtype_bytes
            me = where[axis]
            if axis == "z":
                name = tag + "z"
                make(t, name, deps, region(me, col, width), region(me, col, width), "zA", bytes_ * width, prio)
                deps = [name]
                blocks *= 2
            else:
                first = (width // T + 1) // 2 * T
                pl_, mi = axis + "+", axis + "-"
                a, b, c, d = (tag + axis + k for k in ("p", "m", "fp", "fm"))
                make(t, a, deps, region(me, col, width), region(me, col, width), pl_, bytes_ * width, prio)
                make(t, b, deps, region(me, col, width), region(me, col, width), mi, bytes_ * width, prio)
                left, right = nxt(axis, -1), nxt(axis, 1)
                make(t, c, [a], region(left, col, first), region(left, col, first), pl_, bytes_ * first, prio)
                deps = [a, b, c]
                if width > first:
                    rc, rw = col + first, width - first
                    make(t, d, [b], region(right, rc, rw), region(right, rc, rw), mi, bytes_ * rw, prio)
                    deps = [a, b, c, d]
                blocks *= RING
            gathered = gathered + (axis,)
        return deps

    n = 2 * zh + core
    n2 = 2 * (1 - zh) + core
    make(t, "g_core", ["ld_g"], gvm.at[n], gvm.at[n], "core", 131072, -9)
    make(t, "g_z2", ["ld_g"], gvm.at[n], gvm.at[n], "z2", 131072, -9)
    make(t, "g_fwd", ["g_z2"], gvm.at[n2], gvm.at[n2], "core", 131072, -9)

    def mul_out():
        g = gvm[...].reshape(4 * 256, 256)

        def step(j, carry):
            c = pl.multiple_of(j * 256, 256)
            v = jnp.dot(g, bovm[:, pl.ds(c, 256)], preferred_element_type=F32)
            qb[:, :, :, :, pl.ds(c, 256)] = v.astype(BF).reshape(2, RING, RING, ROWS, 256)
            return carry
        lax.fori_loop(0, 8, step, 0)
    t.add("mul_out", ["g_core", "g_z2", "g_fwd", "ld_bo"], mul_out, "compute", cost=3.0, prio=-9)

    out_ready = []
    for p, order in enumerate(OUT_REDUCE):
        u, v = order[0], order[1]
        base = p * 1024
        t1, t2, u1, u2, r1, v1, v2, w1, w2, r2, z1 = rs[p]
        prio = -8 + p * 0.1

        def qreg(at, c, w, u=u):
            i = (slice(None), at, slice(None)) if u == "y" else (slice(None), slice(None), at)
            return i + (slice(None), pl.ds(c, w))
        me, right, left, far = where[u], nxt(u, 1), nxt(u, -1), nxt(u, 2)
        k = "r%d" % p
        big = 8 * ROWS * 2
        make(t, k + "a", ["mul_out"], qb.at[qreg(far, base, 512)], t1, u + "+", big * 512, prio)
        make(t, k + "b", ["mul_out"], qb.at[qreg(far, base + 512, 512)], t2, u + "-", big * 512, prio)

        def acc(at, c, t_, qreg=qreg):
            def run():
                for zz in range(2):
                    i = qreg(at, c, 512)
                    i = (zz,) + i[1:]
                    qb[i] = (qb[i].astype(F32) + t_[zz].astype(F32)).astype(BF)
            return run
        t.add(k + "aa", [k + "a"], acc(right, base, t1), "compute", cost=0.5, prio=prio)
        make(t, k + "c", [k + "aa"], qb.at[qreg(right, base, 1024)], u1, u + "+", big * 1024, prio)
        t.add(k + "bb", [k + "b"], acc(left, base + 512, t2), "compute", cost=0.5, prio=prio)
        make(t, k + "d", [k + "bb"], qb.at[qreg(left, base, 1024)], u2, u + "-", big * 1024, prio)

        def sum1(qreg=qreg, me=me, base=base, r1=r1, u1=u1, u2=u2):
            for zz in range(2):
                i = (zz,) + qreg(me, base, 1024)[1:]
                r1[zz] = qb[i].astype(F32) + u1[zz].astype(F32) + u2[zz].astype(F32)
        t.add(k + "s", [k + "c", k + "d"], sum1, "compute", cost=1.0, prio=prio)

        me, right, left, far = where[v], nxt(v, 1), nxt(v, -1), nxt(v, 2)
        mid = 2 * ROWS * 4
        make(t, k + "e", [k + "s"], r1.at[:, far, :, pl.ds(0, 512)], v1, v + "+", mid * 512, prio)
        make(t, k + "f", [k + "s"], r1.at[:, far, :, pl.ds(512, 512)], v2, v + "-", mid * 512, prio)

        def acc2(at, c, t_, r1=r1):
            def run():
                r1[:, at, :, pl.ds(c, 512)] += t_[...]
            return run
        t.add(k + "ee", [k + "e"], acc2(right, 0, v1), "compute", cost=0.3, prio=prio)
        make(t, k + "g", [k + "ee"], r1.at[:, right], w1, v + "+", mid * 1024, prio)
        t.add(k + "ff", [k + "f"], acc2(left, 512, v2), "compute", cost=0.3, prio=prio)
        make(t, k + "h", [k + "ff"], r1.at[:, left], w2, v + "-", mid * 1024, prio)

        def sum2(r1=r1, me=me, w1=w1, w2=w2, r2=r2):
            r2[...] = r1[:, me] + w1[...] + w2[...]
        t.add(k + "t", [k + "g", k + "h"], sum2, "compute", cost=0.3, prio=prio)
        make(t, k + "i", [k + "t"], r2.at[1 - z], z1, "zA", ROWS * 1024 * 4, prio)

        def sum3(r2=r2, z1=z1, base=base):
            ro[z, y, x, :, pl.ds(base, 1024)] = (r2[z] + z1[...]).astype(BF)
        t.add(k + "u", [k + "i"], sum3, "compute", cost=0.3, prio=prio)
        out_ready += gather("o%d" % p, ro, 2, ROWS, base, 1024, OUT_GATHER[p], [k + "u"], 50 + p)

    rlay = [[pl.ds(0, 64), pl.ds(64, 64)]] * 2
    fin = []
    for h in range(2):
        hp = 10.0 * h
        ab = abuf.at[h]
        col, muls = 0, []
        for j, (tiles, order) in enumerate(PIECES[h]):
            width = tiles * T
            tag = "a%d%d" % (h, j)
            deps = gather(tag, ab, 2, HALF, col, width, order, ["ld_a"], hp + j * 0.1)

            def mul(col=col, width=width, first=(j == 0), h=h):
                def step(s, carry):
                    v = jnp.dot(
                        abuf[h, s, :, :, :, pl.ds(col, width)].reshape(256, width),
                        bvm[pl.ds(col, width), :],
                        preferred_element_type=F32,
                    )
                    if first:
                        part[h, s] = v
                    else:
                        part[h, s] += v
                    return carry
                lax.fori_loop(0, 2, step, 0)
            prev = [muls[-1]] if muls else []
            t.add(tag + "mul", deps + prev + ["ld_b"], mul, "compute", cost=tiles * 0.19, prio=hp + j)
            muls.append(tag + "mul")
            col += width
        e1, e2, ra, rb, r3a, r3b = ex[h]
        k = "e%d" % h
        hp = 20 + h
        make(t, k + "c", [muls[-1]], part.at[h, 1 - core], e1, "core", 256 * 896 * 4, hp)

        def add1(h=h, e1=e1):
            part[h, core] += e1[...]
        t.add(k + "s", [k + "c"], add1, "compute", cost=0.5, prio=hp)
        theirs = (1 - zh) * 128
        mine = zh * 128
        make(t, k + "a", [k + "s"], part.at[h, core, pl.ds(theirs, 64)], ra, "zA", 64 * 896 * 4, hp)
        make(t, k + "b", [k + "s"], part.at[h, core, pl.ds(theirs + 64, 64)], rb, "zB", 64 * 896 * 4, hp)
        make(t, k + "ra", [k + "a"], ra, e2.at[pl.ds(0, 64)], "zB", 64 * 896 * 4, hp)
        make(t, k + "rb", [k + "b"], rb, e2.at[pl.ds(64, 64)], "zA", 64 * 896 * 4, hp)

        def add2(h=h, e2=e2):
            ri[h, core, pl.ds(zh * 8, 8)] = (part[h, core, pl.ds(mine, 128)] + e2[...]).astype(BF).reshape(8, 16, 896)
        t.add(k + "t", [k + "ra", k + "rb"], add2, "compute", cost=0.3, prio=hp)
        m8, t8 = zh * 8, (1 - zh) * 8
        make(t, k + "d", [k + "t"], ri.at[h, core, pl.ds(m8, 4)], r3a, "zA", 64 * 896 * 2, hp)
        make(t, k + "e", [k + "t"], ri.at[h, core, pl.ds(m8 + 4, 4)], r3b, "zB", 64 * 896 * 2, hp)
        make(t, k + "f", [k + "t"], ri.at[h, core, pl.ds(m8, 8)], ri.at[h, core, pl.ds(m8, 8)], "core", 128 * 896 * 2, hp)
        make(t, k + "rd", [k + "d"], r3a, ri.at[h, core, pl.ds(m8, 4)], "zB", 64 * 896 * 2, hp)
        make(t, k + "re", [k + "e"], r3b, ri.at[h, core, pl.ds(t8 + 4, 4)], "zA", 64 * 896 * 2, hp)
        make(t, k + "g", [k + "rd", k + "re"], ri.at[h, core, pl.ds(t8, 8)], ri.at[h, core, pl.ds(t8, 8)], "core", 128 * 896 * 2, hp)
        fin += [k + "f", k + "g", k + "rd", k + "re"]
    return out_ready, fin


def rotate_kernel(acts, grads, bin_, bout, ri_out, ro_out, *scratch):
    (abuf, bvm, part, qb, ro, ri, gvm, bovm), rest = scratch[:8], scratch[8:]
    rs = [rest[0:11], rest[11:22]]
    ex = [rest[22:28], rest[28:34]]
    ssem, rsem, lsem = rest[34:]
    w, n = lax.axis_index("wide"), lax.axis_index("narrow")
    z, y, x = w // 16, (w // 4) % 4, w % 4
    zh, core = n // 2, n % 2
    where = dict(x=x, y=y, z=z, zh=zh, core=core)

    def dev(z_, y_, x_, zh_, core_):
        return {"wide": z_ * 16 + y_ * 4 + x_, "narrow": zh_ * 2 + core_}

    ring = lambda v, d: lax.rem(v + (RING + d), RING)
    peers = {
        "x+": dev(z, y, ring(x, 1), zh, core),
        "x-": dev(z, y, ring(x, -1), zh, core),
        "y+": dev(z, ring(y, 1), x, zh, core),
        "y-": dev(z, ring(y, -1), x, zh, core),
        "zA": dev(1 - z, y, x, zh, core),
        "zB": dev(1 - z, y, x, 1 - zh, core),
        "z2": dev(z, y, x, 1 - zh, core),
        "core": dev(z, y, x, zh, 1 - core),
    }

    local = {}

    def load(name, src, dst):
        c = pltpu.make_async_copy(src, dst, lsem.at[len(local)])
        c.start()
        local[name] = c

    for h in range(2):
        load("a%d" % h, acts.at[pl.ds(h * HALF, HALF)], abuf.at[h, z, y, x])
    load("g", grads, gvm.at[n])
    load("bo", bout, bovm)
    load("b", bin_, bvm)

    barrier = pltpu.get_barrier_semaphore()
    for p in peers.values():
        pl.semaphore_signal(barrier, inc=1, device_id=p, device_id_type=MESH)
    pl.semaphore_wait(barrier, len(peers))

    t = Tasks()
    copies = {}

    def make(t, name, deps, src, dst, link, nbytes, prio):
        i = len(copies)
        copies[name] = (i, src, dst, link)

        def emit():
            d = pltpu.make_async_remote_copy(
                src_ref=src, dst_ref=dst, send_sem=ssem.at[i], recv_sem=rsem.at[i],
                device_id=peers[link], device_id_type=MESH)
            d.start()
            return d
        cost = nbytes / (RATE * (6 if link == "core" else 1))
        t.add(name, deps, emit, "send", link, cost, prio)

    t.add("ld_a", [], lambda: (local.pop("a0").wait(), local.pop("a1").wait()), "compute", cost=0.5, prio=-10)
    t.add("ld_g", [], lambda: local.pop("g").wait(), "compute", cost=0.3, prio=-11)
    t.add("ld_bo", [], lambda: local.pop("bo").wait(), "compute", cost=0.5, prio=-9)
    t.add("ld_b", [], lambda: local.pop("b").wait(), "compute", cost=2.0, prio=-8.9)

    refs = (acts, grads, bin_, bout, ri_out, ro_out, abuf, bvm, part, qb, ro, rs, ex, ri, gvm, bovm, lsem)
    out_ready, fin = build(t, refs, where, make)

    started, arrived = {}, set()

    def need(name):
        if name in copies and name not in arrived:
            started[name].wait_recv()
            arrived.add(name)

    for i in t.order()[0]:
        name, deps, emit, kind, link, cost, prio = t.items[i]
        for d in deps:
            need(d)
        r = emit()
        if kind == "send":
            started[name] = r
    for name in copies:
        need(name)
    for name in copies:
        started[name].wait_send()
    outs = [pltpu.make_async_copy(ro, ro_out, lsem.at[5])]
    for h in range(2):
        for s in range(2):
            outs.append(pltpu.make_async_copy(
                ri.at[h, s], ri_out.at[s, :, h], lsem.at[6 + 2 * h + s]))
    for c in outs:
        c.start()
    for c in outs:
        c.wait()


def rotate(acts, grads, bin_, bout):
    V = pltpu.VMEM
    scratch = [
        V((2, 2, RING, RING, HALF, 7168), BF),
        V((7168, 896), BF),
        V((2, 2, 256, 896), F32),
        V((2, RING, RING, ROWS, 2048), BF),
        V((2, RING, RING, ROWS, 2048), BF),
        V((2, 2, 16, 16, 896), BF),
        V((4, 256, 256), BF),
        V((256, 2048), BF),
    ]
    for p in range(2):
        scratch += [V((2, RING, ROWS, 512), BF)] * 2
        scratch += [V((2, RING, ROWS, 1024), BF)] * 2
        scratch += [V((2, RING, ROWS, 1024), F32)]
        scratch += [V((2, ROWS, 512), F32)] * 2
        scratch += [V((2, ROWS, 1024), F32)] * 3
        scratch += [V((ROWS, 1024), F32)]
    for h in range(2):
        scratch += [V((256, 896), F32), V((128, 896), F32), V((64, 896), F32), V((64, 896), F32)]
        scratch += [V((4, 16, 896), BF), V((4, 16, 896), BF)]
    count = 160
    scratch += [pltpu.SemaphoreType.DMA((count,)), pltpu.SemaphoreType.DMA((count,)), pltpu.SemaphoreType.DMA((10,))]
    any_ = pl.BlockSpec(memory_space=pl.ANY)
    return pl.pallas_call(
        rotate_kernel,
        out_shape=(
            jax.ShapeDtypeStruct((2, 16, 2, 256 // 16, 896), BF),
            jax.ShapeDtypeStruct((2, RING, RING, ROWS, 2048), BF),
        ),
        in_specs=[any_] * 4,
        out_specs=[any_] * 2,
        scratch_shapes=scratch,
        compiler_params=pltpu.CompilerParams(
            collective_id=0, has_side_effects=True, vmem_limit_bytes=67043328),
        name="rotate",
    )(acts, grads, bin_, bout)


def final_kernel(ro_ref, ri_ref, o_ref):
    total = None
    for s in range(SEQS):
        r = lax.dot_general(
            ro_ref[pl.ds(s * 512, 512), :], ri_ref[pl.ds(s * 512, 512), :],
            (((0,), (0,)), ((), ())), preferred_element_type=F32)
        total = r * r if total is None else total + r * r
    o_ref[...] = total * (1.0 / SEQS)


def final(ro, ri):
    tile = 256
    return pl.pallas_call(
        final_kernel,
        grid=(2048 // tile,),
        in_specs=[pl.BlockSpec((1024, tile), lambda i: (0, i)), pl.BlockSpec((1024, 896), lambda i: (0, 0))],
        out_specs=pl.BlockSpec((tile, 896), lambda i: (i, 0)),
        out_shape=jax.ShapeDtypeStruct((2048, 896), F32),
        name="final",
    )(ro, ri)


def body(activations, out_grads, basis_in, basis_out):
    ri, ro = rotate(activations, out_grads, basis_in, basis_out)
    return final(ro.reshape(1024, 2048), ri.reshape(1024, 896))


def solution(mesh):
    in_specs = (P("wide", "narrow"), P("narrow", "wide"), P("narrow", "wide"), P("wide", "narrow"))
    return jax.shard_map(body, mesh=mesh, in_specs=in_specs, out_specs=P("narrow", "wide"), check_vma=False)
```

```python
import functools

import jax
import jax.numpy as jnp
from jax import lax
from jax.experimental import pallas as pl
from jax.experimental.pallas import tpu as pltpu
from jax.sharding import PartitionSpec as P

MESH = pl.DeviceIdType.MESH
BF, F32 = jnp.bfloat16, jnp.float32
SEQS = 2
ROWS = 32
HALF = 16
RING = 4
T = 128

PIECES = (
    ((10, "zxy"), (8, "zyx"), (10, "zxy"), (8, "zyx"), (5, "xyz"), (5, "yxz"), (5, "xyz"), (5, "yxz")),
    ((8, "zxy"), (6, "zyx"), (8, "zxy"), (6, "zyx"), (8, "zxy"), (6, "zyx"), (7, "xyz"), (7, "yxz")),
)
OUT_GATHER = ((0, 64, 0, 256, "zxy"), (0, 64, 256, 256, "zyx"), (64, 64, 0, 256, "zyx"), (64, 64, 256, 256, "zxy"),)
ORDER = (
    2, 3, 0, 135, 134, 74, 94, 223, 64, 203, 224, 115, 114, 183, 1, 84, 8, 104, 105, 137, 136, 124, 125, 75, 76, 226, 225, 213, 214,
    117, 116, 95, 96, 4, 5, 153, 204, 205, 193, 184, 185, 163, 173, 77, 85, 86, 78, 106, 107, 98, 127, 126, 97, 119, 215, 118, 207,
    206, 195, 187, 186, 9, 165, 164, 7, 108, 109, 128, 129, 167, 166, 88, 121, 216, 139, 87, 110, 111, 174, 197, 194, 10, 130, 131,
    227, 112, 217, 218, 89, 90, 120, 65, 141, 66, 132, 196, 138, 155, 229, 219, 220, 228, 11, 113, 198, 199, 12, 67, 122, 140, 68,
    6, 175, 92, 91, 230, 208, 133, 100, 13, 69, 70, 221, 99, 14, 177, 80, 123, 201, 200, 93, 79, 16, 15, 102, 231, 72, 71, 209, 101,
    202, 222, 176, 154, 19, 20, 82, 17, 18, 210, 157, 142, 168, 169, 73, 178, 179, 103, 156, 232, 211, 81, 21, 22, 189, 188, 159,
    158, 171, 212, 170, 143, 180, 181, 83, 144, 145, 191, 190, 23, 24, 34, 44, 161, 160, 54, 146, 147, 172, 182, 35, 46, 45, 25, 36,
    26, 192, 55, 56, 162, 233, 37, 48, 27, 28, 47, 38, 57, 58, 234, 238, 29, 30, 50, 39, 59, 60, 235, 148, 40, 150, 49, 149, 31, 32,
    239, 240, 52, 41, 61, 62, 236, 237, 42, 51, 33, 241, 151, 63, 43, 53, 152,
)


class Tasks:
    def __init__(self):
        self.items = {}

    def add(self, name, deps, emit, kind, link=None, cost=0.0):
        self.items[name] = (name, tuple(deps), emit, kind, link, cost)


def ax_index(axis, where, at, gathered):
    return slice(None) if axis in gathered else at.get(axis, where[axis])


def build(t, refs, where, make, write, loaded):
    bout, abuf, bvm, part, ro, rs, ex, ri = refs
    x, y, z, zh, core = (where[k] for k in ("x", "y", "z", "zh", "core"))

    def nxt(axis, d):
        return lax.rem(where[axis] + (RING + d), RING)

    def gather(tag, buf, dtype_bytes, rows, col, width, order, deps, part_rows=slice(None)):
        gathered = ()
        blocks = 1
        for axis in order:
            def region(at, c, w, gathered=gathered, axis=axis):
                i = tuple(ax_index(a, where, {axis: at}, gathered) for a in "zyx")
                return buf.at[i + (part_rows, pl.ds(c, w))]
            bytes_ = blocks * rows * dtype_bytes
            me = where[axis]
            if axis == "z":
                name = tag + "z"
                make(t, name, deps, region(me, col, width), region(me, col, width), "zA", bytes_ * width)
                deps = [name]
                blocks *= 2
            else:
                first = (width // T + 1) // 2 * T
                pl_, mi = axis + "+", axis + "-"
                a, b, c, d = (tag + axis + k for k in ("p", "m", "fp", "fm"))
                make(t, a, deps, region(me, col, width), region(me, col, width), pl_, bytes_ * width)
                make(t, b, deps, region(me, col, width), region(me, col, width), mi, bytes_ * width)
                left, right = nxt(axis, -1), nxt(axis, 1)
                make(t, c, [a], region(left, col, first), region(left, col, first), pl_, bytes_ * first)
                deps = [a, b, c]
                if width > first:
                    rc, rw = col + first, width - first
                    make(t, d, [b], region(right, rc, rw), region(right, rc, rw), mi, bytes_ * rw)
                    deps = [a, b, c, d]
                blocks *= RING
            gathered = gathered + (axis,)
        return deps

    bo4, bora, borb, g4, qb, t1, t2, u1, u2, r1, z1, qf = rs
    bov = [bout.at[:, pl.ds(pl.multiple_of(lax.rem(x + k, RING) * 512, 512), 512)] for k in range(RING)]
    left, right, far = nxt("x", -1), nxt("x", 1), nxt("x", 2)
    blk = 256 * 512 * 2
    make(t, "bp", [], bov[1], bo4.at[x], "x+", blk)
    make(t, "bm", [], bov[3], bo4.at[x], "x-", blk)
    make(t, "bfp", [], bov[2].at[pl.ds(0, 128)], bora, "x+", blk // 2)
    make(t, "bfm", [], bov[2].at[pl.ds(128, 128)], borb, "x-", blk // 2)
    make(t, "brp", ["bfp"], bora, bo4.at[left, pl.ds(0, 128)], "x+", blk // 2)
    make(t, "brm", ["bfm"], borb, bo4.at[right, pl.ds(128, 128)], "x-", blk // 2)
    gblk = 256 * 256 * 2
    make(t, "gz", ["ld_g"], g4.at[x, zh, core], g4.at[x, zh, core], "z2", gblk)
    mine, both = g4.at[x, :, core], g4.at[:, :, core]
    make(t, "gp", ["gz"], mine, mine, "x+", 2 * gblk)
    make(t, "gm", ["gz"], mine, mine, "x-", 2 * gblk)
    make(t, "gfp", ["gp"], g4.at[left, 0, core], g4.at[left, 0, core], "x+", gblk)
    make(t, "gfm", ["gm"], g4.at[right, 1, core], g4.at[right, 1, core], "x-", gblk)
    make(t, "gc", ["gp", "gm", "gfp", "gfm"], both, both, "core", 8 * gblk)

    def mul_out():
        loaded("bo")

        def step(i, carry):
            a, b = i // 2, i % 2
            v = None
            for k in range(RING):
                d = jnp.dot(g4[k, a, b], bo4[k], preferred_element_type=F32)
                v = d if v is None else v + d
            v = v.reshape(2, RING, ROWS, 512)
            qf[a, pl.ds(b * 2, 2)] = v
            qb[a, pl.ds(b * 2, 2)] = v.astype(BF)
            return carry
        lax.fori_loop(0, 4, step, 0)
    t.add("mo", ["gc", "bp", "bm", "brp", "brm"], mul_out, "compute", cost=3.0)

    left, right, far = nxt("y", -1), nxt("y", 1), nxt("y", 2)
    big = 8 * ROWS * 2
    lo, hi = pl.ds(0, 256), pl.ds(256, 256)
    make(t, "ra", ["mo"], qb.at[:, far, :, :, lo], t1, "y+", big * 256)
    make(t, "rb", ["mo"], qb.at[:, far, :, :, hi], t2, "y-", big * 256)

    def acc(at, c, t_):
        def run():
            qb[:, at, :, :, c] = (qf[:, at, :, :, c] + t_[...].astype(F32)).astype(BF)
        return run
    t.add("raa", ["ra"], acc(right, lo, t1), "compute", cost=0.5)
    make(t, "rc", ["raa"], qb.at[:, right], u1, "y+", big * 512)
    t.add("rbb", ["rb"], acc(left, hi, t2), "compute", cost=0.5)
    make(t, "rd", ["rbb"], qb.at[:, left], u2, "y-", big * 512)

    def sum1():
        r1[...] = qf[:, y] + u1[...].astype(F32) + u2[...].astype(F32)
    t.add("rs", ["rc", "rd"], sum1, "compute", cost=0.8)
    make(t, "rz", ["rs"], r1.at[1 - z], z1, "zA", 128 * 512 * 4)

    def sum2():
        ro[z, y, x] = (r1[z] + z1[...]).astype(BF).reshape(128, 512)
    t.add("rt", ["rz"], sum2, "compute", cost=0.4)
    for p, (row, rows, col, width, order) in enumerate(OUT_GATHER):
        deps = gather("o%d" % p, ro, 2, rows, col, width, order, ["rt"], pl.ds(row, rows))
        t.add("v%d" % p, deps, lambda p=p: write("ro", p), "compute", cost=0.1)

    begun = set()
    for h in range(2):
        ab = abuf.at[h]
        col, muls = 0, []
        for j, (tiles, order) in enumerate(PIECES[h]):
            width = tiles * T
            tag = "a%d%d" % (h, j)
            deps = gather(tag, ab, 2, HALF, col, width, order, ["ld_a"])

            def mul(col=col, width=width, h=h):
                loaded("b")
                first = h not in begun
                begun.add(h)

                def step(s, carry):
                    v = jnp.dot(
                        abuf[h, s, :, :, :, pl.ds(col, width)].reshape(256, width),
                        bvm[pl.ds(col, width), :],
                        preferred_element_type=F32,
                    ).reshape(16, 16, 896)
                    if first:
                        part[h, s] = v
                    else:
                        part[h, s] += v
                    return carry
                lax.fori_loop(0, 2, step, 0)
            t.add(tag + "mul", deps, mul, "compute", cost=tiles * 0.17)
            muls.append(tag + "mul")
            col += width
        k = "e%d" % h
        m8, t8 = pl.ds(zh * 8, 8), pl.ds((1 - zh) * 8, 8)
        wide_, thin = 8 * 16 * 896 * 4, 8 * 16 * 896 * 2

        if h == 0:
            e1, e2 = ex[0]
            make(t, k + "x", muls, part.at[h, 1 - core, t8], e1.at[t8], "core", wide_)
            make(t, k + "y", muls, part.at[h, 1 - core, m8], e1.at[m8], "core", wide_)

            def add1(h=h, e1=e1, t8=t8):
                part[h, core, t8] += e1[t8]
            t.add(k + "s", [k + "x"], add1, "compute", cost=0.3)
            make(t, k + "a", [k + "s"], part.at[h, core, t8], e2, "z2", wide_)

            def add2(h=h, e1=e1, e2=e2, m8=m8):
                ri[h, core, m8] = (part[h, core, m8] + e1[m8] + e2[...]).astype(BF)
            t.add(k + "t", [k + "a", k + "y"], add2, "compute", cost=0.4)
            mine = ri.at[h, core, m8]
            make(t, k + "d", [k + "t"], mine, mine, "z2", thin)
            make(t, k + "f", [k + "t"], mine, mine, "core", thin)
            make(t, k + "g", [k + "d"], ri.at[h, core, t8], ri.at[h, core, t8], "core", thin)
            t.add("w%d" % h, [k + "d", k + "f", k + "g"], lambda h=h: write("ri", h), "compute", cost=0.1)
        else:
            e1, eb, er = ex[1]
            make(t, k + "x", muls, part.at[h, 1 - core], e1, "core", 2 * wide_)

            def add1(h=h, e1=e1, eb=eb):
                v = part[h, core] + e1[...]
                part[h, core] = v
                eb[...] = v.astype(BF)
            t.add(k + "s", [k + "x"], add1, "compute", cost=0.5)
            done = []
            for i in range(2):
                c, rows = k + str(i), pl.ds(i * 8, 8)
                make(t, c + "a", [k + "s"], eb.at[rows], er.at[rows], "z2", thin)

                def add2(h=h, er=er, rows=rows):
                    ri[h, core, rows] = (part[h, core, rows] + er[rows].astype(F32)).astype(BF)
                t.add(c + "t", [c + "a"], add2, "compute", cost=0.2)
                mine = ri.at[h, core, rows]
                make(t, c + "f", [c + "t"], mine, mine, "core", thin)
                done += [c + "t", c + "f"]
            t.add("w%d" % h, done, lambda h=h: write("ri", h), "compute", cost=0.1)
    return


def rotate_kernel(acts, grads, bin_, bout, ri_out, ro_out, *scratch):
    (abuf, bvm, part, ro, ri), rest = scratch[:5], scratch[5:]
    rs = rest[0:12]
    ex = [rest[12:14], rest[14:17]]
    ssem, rsem, lsem = rest[17:]
    bo4, g4 = rs[0], rs[3]
    w, n = lax.axis_index("wide"), lax.axis_index("narrow")
    z, y, x = w // 16, (w // 4) % 4, w % 4
    zh, core = n // 2, n % 2
    where = dict(x=x, y=y, z=z, zh=zh, core=core)

    def dev(z_, y_, x_, zh_, core_):
        return {"wide": z_ * 16 + y_ * 4 + x_, "narrow": zh_ * 2 + core_}

    ring = lambda v, d: lax.rem(v + (RING + d), RING)
    peers = {
        "x+": dev(z, y, ring(x, 1), zh, core),
        "x-": dev(z, y, ring(x, -1), zh, core),
        "y+": dev(z, ring(y, 1), x, zh, core),
        "y-": dev(z, ring(y, -1), x, zh, core),
        "zA": dev(1 - z, y, x, zh, core),
        "zB": dev(1 - z, y, x, 1 - zh, core),
        "z2": dev(z, y, x, 1 - zh, core),
        "core": dev(z, y, x, zh, 1 - core),
    }

    local = {}

    def load(name, src, dst):
        c = pltpu.make_async_copy(src, dst, lsem.at[len(local)])
        c.start()
        local[name] = c

    for h in range(2):
        load("a%d" % h, acts.at[pl.ds(h * HALF, HALF)], abuf.at[h, z, y, x])
    load("g", grads, g4.at[x, zh, core])
    load("bo", bout.at[:, pl.ds(pl.multiple_of(x * 512, 512), 512)], bo4.at[x])
    load("b", bin_, bvm)

    barrier = pltpu.get_barrier_semaphore()
    for p in peers.values():
        pl.semaphore_signal(barrier, inc=1, device_id=p, device_id_type=MESH)
    pl.semaphore_wait(barrier, len(peers))

    t = Tasks()
    copies = {}

    def make(t, name, deps, src, dst, link, nbytes):
        i = len(copies)
        copies[name] = (i, src, dst, link)

        def emit():
            d = pltpu.make_async_remote_copy(
                src_ref=src, dst_ref=dst, send_sem=ssem.at[i], recv_sem=rsem.at[i],
                device_id=peers[link], device_id_type=MESH)
            d.start()
            return d
        t.add(name, deps, emit, "send", link, nbytes)

    def loaded(*names):
        for name in names:
            if name in local:
                local.pop(name).wait()

    t.add("ld_a", [], lambda: loaded("a0", "a1"), "compute", cost=0.5)
    t.add("ld_g", [], lambda: loaded("g"), "compute", cost=0.3)

    refs = (bout, abuf, bvm, part, ro, rs, ex, ri)
    outs = []

    def write(what, i):
        if what == "ro":
            row, rows, col, width, _ = OUT_GATHER[i]
            c = (slice(None),) * 3 + (pl.ds(row, rows), pl.ds(col, width))
            pairs = [(ro.at[c], ro_out.at[c])]
        else:
            pairs = [(ri.at[i, s], ri_out.at[s, :, i]) for s in range(SEQS)]
        for src, dst in pairs:
            c = pltpu.make_async_copy(src, dst, lsem.at[4 + len(outs)])
            c.start()
            outs.append(c)

    build(t, refs, where, make, write, loaded)

    started, arrived = {}, set()

    def need(name):
        if name in copies and name not in arrived:
            started[name].wait_recv()
            arrived.add(name)

    names = list(t.items)
    assert sorted(ORDER) == list(range(len(names)))
    for name in [names[i] for i in ORDER]:
        _, deps, emit, kind, _, _ = t.items[name]
        for d in deps:
            need(d)
        r = emit()
        if kind == "send":
            started[name] = r
    for name in copies:
        need(name)
    for name in copies:
        started[name].wait_send()
    for c in outs:
        c.wait()


def rotate(acts, grads, bin_, bout):
    V = pltpu.VMEM
    scratch = [
        V((2, 2, RING, RING, HALF, 7168), BF),
        V((7168, 896), BF),
        V((2, 2, 16, 16, 896), F32),
        V((2, RING, RING, 128, 512), BF),
        V((2, 2, 16, 16, 896), BF),
        V((RING, 256, 512), BF), V((128, 512), BF), V((128, 512), BF),
        V((RING, 2, 2, 256, 256), BF),
        V((2, RING, RING, ROWS, 512), BF),
        V((2, RING, ROWS, 256), BF), V((2, RING, ROWS, 256), BF),
        V((2, RING, ROWS, 512), BF), V((2, RING, ROWS, 512), BF),
        V((2, RING, ROWS, 512), F32), V((RING, ROWS, 512), F32),
        V((2, RING, RING, ROWS, 512), F32),
    ]
    scratch += [V((16, 16, 896), F32), V((8, 16, 896), F32)]
    scratch += [V((16, 16, 896), F32), V((16, 16, 896), BF), V((16, 16, 896), BF)]
    count = 240
    scratch += [pltpu.SemaphoreType.DMA((count,)), pltpu.SemaphoreType.DMA((count,)), pltpu.SemaphoreType.DMA((16,))]
    any_ = pl.BlockSpec(memory_space=pl.ANY)
    return pl.pallas_call(
        rotate_kernel,
        out_shape=(
            jax.ShapeDtypeStruct((2, 16, 2, 256 // 16, 896), BF),
            jax.ShapeDtypeStruct((2, RING, RING, 128, 512), BF),
        ),
        in_specs=[any_] * 4,
        out_specs=[any_] * 2,
        scratch_shapes=scratch,
        compiler_params=pltpu.CompilerParams(
            collective_id=0, has_side_effects=True, vmem_limit_bytes=67043328),
        name="rotate",
    )(acts, grads, bin_, bout)


def final_kernel(ro_ref, ri_ref, o_ref):
    total = None
    for s in range(SEQS):
        r = lax.dot_general(
            ro_ref[s].reshape(512, -1), ri_ref[pl.ds(s * 512, 512), :],
            (((0,), (0,)), ((), ())), preferred_element_type=F32)
        total = r * r if total is None else total + r * r
    o_ref[...] = total * (1.0 / SEQS)


def final(ro, ri):
    tile = 512
    return pl.pallas_call(
        final_kernel,
        grid=(2048 // tile,),
        in_specs=[
            pl.BlockSpec((2, RING, None, 128, tile), lambda i: (0, 0, i, 0, 0)),
            pl.BlockSpec((1024, 896), lambda i: (0, 0)),
        ],
        out_specs=pl.BlockSpec((tile, 896), lambda i: (i, 0)),
        out_shape=jax.ShapeDtypeStruct((2048, 896), F32),
        name="final",
    )(ro, ri)


def body(activations, out_grads, basis_in, basis_out):
    ri, ro = rotate(activations, out_grads, basis_in, basis_out)
    return final(ro, ri.reshape(1024, 896))


def solution(mesh):
    in_specs = (P("wide", "narrow"), P("narrow", "wide"), P("narrow", "wide"), P("wide", "narrow"))
    return jax.shard_map(body, mesh=mesh, in_specs=in_specs, out_specs=P("narrow", "wide"), check_vma=False)
```

```python
import functools

import jax
import jax.numpy as jnp
from jax import lax
from jax.experimental import pallas as pl
from jax.experimental.pallas import tpu as pltpu
from jax.sharding import PartitionSpec as P

MESH = pl.DeviceIdType.MESH
BF, F32 = jnp.bfloat16, jnp.float32
SEQS = 2
ROWS = 32
HALF = 16
RING = 4
T = 128

PIECES = (
    ((9, "zxy"), (8, "zyx"), (9, "zxy"), (8, "zyx"), (5, "xyz"), (6, "yxz"), (5, "xyz"), (6, "yxz")),
    ((8, "zxy"), (6, "zyx"), (8, "zxy"), (6, "zyx"), (8, "zxy"), (6, "zyx"), (7, "xyz"), (7, "yxz")),
)
OUT_GATHER = ((0, 64, 0, 256, "zxy"), (0, 64, 256, 256, "zyx"), (64, 64, 0, 256, "zyx"), (64, 64, 256, 256, "zxy"),)
ORDER = (
    4, 5, 0, 115, 94, 138, 167, 217, 105, 84, 229, 116, 207, 137, 187, 228, 127, 104, 1, 8, 218, 126, 2, 3, 117, 140, 95, 96, 139,
    231, 168, 169, 74, 230, 118, 64, 208, 209, 189, 188, 197, 177, 97, 157, 98, 106, 107, 86, 85, 170, 171, 75, 76, 129, 128, 120,
    219, 210, 211, 9, 190, 191, 179, 108, 109, 220, 10, 77, 78, 131, 130, 87, 110, 111, 178, 222, 221, 141, 132, 133, 88, 181, 112,
    11, 122, 113, 66, 224, 223, 180, 199, 119, 89, 90, 12, 135, 6, 7, 182, 183, 65, 225, 114, 201, 121, 142, 232, 13, 68, 226, 100,
    172, 91, 92, 14, 67, 185, 184, 234, 123, 144, 16, 143, 159, 15, 198, 80, 93, 69, 124, 70, 192, 227, 186, 79, 19, 102, 146, 17,
    20, 18, 161, 233, 145, 125, 200, 158, 82, 99, 72, 71, 134, 193, 203, 202, 21, 22, 160, 147, 81, 235, 173, 73, 101, 136, 162,
    163, 195, 237, 194, 83, 212, 213, 205, 23, 204, 34, 103, 54, 148, 44, 24, 175, 174, 196, 165, 236, 164, 36, 149, 55, 56, 35, 46,
    215, 214, 45, 153, 206, 26, 25, 176, 166, 58, 57, 38, 37, 238, 150, 48, 47, 216, 28, 27, 239, 39, 59, 40, 60, 154, 155, 240, 241,
    29, 50, 49, 30, 244, 151, 152, 61, 42, 62, 41, 156, 242, 243, 31, 52, 51, 32, 63, 43, 245, 246, 33, 53, 247,
)


class Tasks:
    def __init__(self):
        self.items = {}

    def add(self, name, deps, emit, kind, link=None, cost=0.0):
        self.items[name] = (name, tuple(deps), emit, kind, link, cost)


def ax_index(axis, where, at, gathered):
    return slice(None) if axis in gathered else at.get(axis, where[axis])


def build(t, refs, where, make, write, loaded):
    bout, abuf, bvm, part, ro, rs, ex, ri = refs
    x, y, z, zh, core = (where[k] for k in ("x", "y", "z", "zh", "core"))

    def nxt(axis, d):
        return lax.rem(where[axis] + (RING + d), RING)

    def gather(tag, buf, dtype_bytes, rows, col, width, order, deps, part_rows=slice(None)):
        gathered = ()
        blocks = 1
        for axis in order:
            def region(at, c, w, gathered=gathered, axis=axis):
                i = tuple(ax_index(a, where, {axis: at}, gathered) for a in "zyx")
                return buf.at[i + (part_rows, pl.ds(c, w))]
            bytes_ = blocks * rows * dtype_bytes
            me = where[axis]
            if axis == "z":
                parts = ((0, width),)
                if blocks > 1:
                    cut = width // T // 2 * T
                    parts = ((0, cut), (cut, width - cut))
                deps_z = []
                for i, (c, w) in enumerate(parts):
                    r = region(me, col + c, w)
                    make(t, tag + "z%d" % i, deps, r, r, "zA", bytes_ * w)
                    deps_z.append(tag + "z%d" % i)
                deps = deps_z
                blocks *= 2
            else:
                first = (width // T + (int(tag[-1]) + 1) % 2) // 2 * T
                pl_, mi = axis + "+", axis + "-"
                a, b, c, d = (tag + axis + k for k in ("p", "m", "fp", "fm"))
                make(t, a, deps, region(me, col, width), region(me, col, width), pl_, bytes_ * width)
                make(t, b, deps, region(me, col, width), region(me, col, width), mi, bytes_ * width)
                left, right = nxt(axis, -1), nxt(axis, 1)
                make(t, c, [a], region(left, col, first), region(left, col, first), pl_, bytes_ * first)
                deps = [a, b, c]
                if width > first:
                    rc, rw = col + first, width - first
                    make(t, d, [b], region(right, rc, rw), region(right, rc, rw), mi, bytes_ * rw)
                    deps = [a, b, c, d]
                blocks *= RING
            gathered = gathered + (axis,)
        return deps

    bo4, bora, borb, g4, qb, t1, t2, u1, u2, r1, z1, qf = rs
    bov = [bout.at[:, pl.ds(pl.multiple_of(lax.rem(x + k, RING) * 512, 512), 512)] for k in range(RING)]
    left, right, far = nxt("x", -1), nxt("x", 1), nxt("x", 2)
    blk = 256 * 512 * 2
    make(t, "bp", [], bov[1], bo4.at[x], "x+", blk)
    make(t, "bm", [], bov[3], bo4.at[x], "x-", blk)
    make(t, "bfp", [], bov[2].at[pl.ds(0, 128)], bora, "x+", blk // 2)
    make(t, "bfm", [], bov[2].at[pl.ds(128, 128)], borb, "x-", blk // 2)
    make(t, "brp", ["bfp"], bora, bo4.at[left, pl.ds(0, 128)], "x+", blk // 2)
    make(t, "brm", ["bfm"], borb, bo4.at[right, pl.ds(128, 128)], "x-", blk // 2)
    gblk = 256 * 256 * 2
    make(t, "gz", ["ld_g"], g4.at[x, zh, core], g4.at[x, zh, core], "z2", gblk)
    mine, both = g4.at[x, :, core], g4.at[:, :, core]
    make(t, "gp", ["gz"], mine, mine, "x+", 2 * gblk)
    make(t, "gm", ["gz"], mine, mine, "x-", 2 * gblk)
    make(t, "gfp", ["gp"], g4.at[left, 0, core], g4.at[left, 0, core], "x+", gblk)
    make(t, "gfm", ["gm"], g4.at[right, 1, core], g4.at[right, 1, core], "x-", gblk)
    make(t, "gc", ["gp", "gm", "gfp", "gfm"], both, both, "core", 8 * gblk)

    def mul_out():
        loaded("bo")

        def step(i, carry):
            a, b = i // 2, i % 2
            v = None
            for k in range(RING):
                d = jnp.dot(g4[k, a, b], bo4[k], preferred_element_type=F32)
                v = d if v is None else v + d
            v = v.reshape(2, RING, ROWS, 512)
            qf[a, pl.ds(b * 2, 2)] = v
            qb[a, pl.ds(b * 2, 2)] = v.astype(BF)
            return carry
        lax.fori_loop(0, 4, step, 0)
    t.add("mo", ["gc", "bp", "bm", "brp", "brm"], mul_out, "compute", cost=3.0)

    left, right, far = nxt("y", -1), nxt("y", 1), nxt("y", 2)
    big = 8 * ROWS * 2
    lo, hi = pl.ds(0, 256), pl.ds(256, 256)
    make(t, "ra", ["mo"], qb.at[:, far, :, :, lo], t1, "y+", big * 256)
    make(t, "rb", ["mo"], qb.at[:, far, :, :, hi], t2, "y-", big * 256)

    def acc(at, c, t_):
        def run():
            qb[:, at, :, :, c] = (qf[:, at, :, :, c] + t_[...].astype(F32)).astype(BF)
        return run
    t.add("raa", ["ra"], acc(right, lo, t1), "compute", cost=0.5)
    make(t, "rc", ["raa"], qb.at[:, right], u1, "y+", big * 512)
    t.add("rbb", ["rb"], acc(left, hi, t2), "compute", cost=0.5)
    make(t, "rd", ["rbb"], qb.at[:, left], u2, "y-", big * 512)

    def sum1():
        r1[...] = qf[:, y] + u1[...].astype(F32) + u2[...].astype(F32)
    t.add("rs", ["rc", "rd"], sum1, "compute", cost=0.8)
    make(t, "rz", ["rs"], r1.at[1 - z], z1, "zA", 128 * 512 * 4)

    def sum2():
        ro[z, y, x] = (r1[z] + z1[...]).astype(BF).reshape(128, 512)
    t.add("rt", ["rz"], sum2, "compute", cost=0.4)
    for p, (row, rows, col, width, order) in enumerate(OUT_GATHER):
        deps = gather("o%d" % p, ro, 2, rows, col, width, order, ["rt"], pl.ds(row, rows))
        t.add("v%d" % p, deps, lambda p=p: write("ro", p), "compute", cost=0.1)

    begun = set()
    for h in range(2):
        ab = abuf.at[h]
        col, muls = 0, []
        for j, (tiles, order) in enumerate(PIECES[h]):
            width = tiles * T
            tag = "a%d%d" % (h, j)
            deps = gather(tag, ab, 2, HALF, col, width, order, ["ld_a"])

            def mul(col=col, width=width, h=h):
                loaded("b")
                first = h not in begun
                begun.add(h)

                def step(s, carry):
                    v = jnp.dot(
                        abuf[h, s, :, :, :, pl.ds(col, width)].reshape(256, width),
                        bvm[pl.ds(col, width), :],
                        preferred_element_type=F32,
                    ).reshape(16, 16, 896)
                    if first:
                        part[h, s] = v
                    else:
                        part[h, s] += v
                    return carry
                lax.fori_loop(0, 2, step, 0)
            t.add(tag + "mul", deps, mul, "compute", cost=tiles * 0.17)
            muls.append(tag + "mul")
            col += width
        k = "e%d" % h
        wide_, thin = 8 * 16 * 896 * 4, 8 * 16 * 896 * 2

        e1, eb, er = ex[h]
        make(t, k + "x", muls, part.at[h, 1 - core], e1, "core", 2 * wide_)

        def add1(h=h, e1=e1, eb=eb):
            v = part[h, core] + e1[...]
            part[h, core] = v
            eb[...] = v.astype(BF)
        t.add(k + "s", [k + "x"], add1, "compute", cost=0.5)
        done = []
        for i in range(2):
            c, rows = k + str(i), pl.ds(i * 8, 8)
            make(t, c + "a", [k + "s"], eb.at[rows], er.at[rows], "z2", thin)

            def add2(h=h, er=er, rows=rows):
                ri[h, core, rows] = (part[h, core, rows] + er[rows].astype(F32)).astype(BF)
            t.add(c + "t", [c + "a"], add2, "compute", cost=0.2)
            mine = ri.at[h, core, rows]
            make(t, c + "f", [c + "t"], mine, mine, "core", thin)
            done += [c + "t", c + "f"]
        t.add("w%d" % h, done, lambda h=h: write("ri", h), "compute", cost=0.1)
    return


def rotate_kernel(acts, grads, bin_, bout, ri_out, ro_out, *scratch):
    (abuf, bvm, part, ro, ri), rest = scratch[:5], scratch[5:]
    rs = rest[0:12]
    ex = [rest[12:15], rest[15:18]]
    ssem, rsem, lsem = rest[18:]
    bo4, g4 = rs[0], rs[3]
    w, n = lax.axis_index("wide"), lax.axis_index("narrow")
    z, y, x = w // 16, (w // 4) % 4, w % 4
    zh, core = n // 2, n % 2
    where = dict(x=x, y=y, z=z, zh=zh, core=core)

    def dev(z_, y_, x_, zh_, core_):
        return {"wide": z_ * 16 + y_ * 4 + x_, "narrow": zh_ * 2 + core_}

    ring = lambda v, d: lax.rem(v + (RING + d), RING)
    peers = {
        "x+": dev(z, y, ring(x, 1), zh, core),
        "x-": dev(z, y, ring(x, -1), zh, core),
        "y+": dev(z, ring(y, 1), x, zh, core),
        "y-": dev(z, ring(y, -1), x, zh, core),
        "zA": dev(1 - z, y, x, zh, core),
        "zB": dev(1 - z, y, x, 1 - zh, core),
        "z2": dev(z, y, x, 1 - zh, core),
        "core": dev(z, y, x, zh, 1 - core),
    }

    local = {}

    def load(name, src, dst):
        c = pltpu.make_async_copy(src, dst, lsem.at[len(local)])
        c.start()
        local[name] = c

    for h in range(2):
        load("a%d" % h, acts.at[pl.ds(h * HALF, HALF)], abuf.at[h, z, y, x])
    load("g", grads, g4.at[x, zh, core])
    load("bo", bout.at[:, pl.ds(pl.multiple_of(x * 512, 512), 512)], bo4.at[x])
    load("b", bin_, bvm)

    barrier = pltpu.get_barrier_semaphore()
    for p in peers.values():
        pl.semaphore_signal(barrier, inc=1, device_id=p, device_id_type=MESH)
    pl.semaphore_wait(barrier, len(peers))

    t = Tasks()
    copies = {}

    def make(t, name, deps, src, dst, link, nbytes):
        i = len(copies)
        copies[name] = (i, src, dst, link)

        def emit():
            d = pltpu.make_async_remote_copy(
                src_ref=src, dst_ref=dst, send_sem=ssem.at[i], recv_sem=rsem.at[i],
                device_id=peers[link], device_id_type=MESH)
            d.start()
            return d
        t.add(name, deps, emit, "send", link, nbytes)

    def loaded(*names):
        for name in names:
            if name in local:
                local.pop(name).wait()

    t.add("ld_a", [], lambda: loaded("a0", "a1"), "compute", cost=0.5)
    t.add("ld_g", [], lambda: loaded("g"), "compute", cost=0.3)

    refs = (bout, abuf, bvm, part, ro, rs, ex, ri)
    outs = []

    def write(what, i):
        if what == "ro":
            row, rows, col, width, _ = OUT_GATHER[i]
            c = (slice(None),) * 3 + (pl.ds(row, rows), pl.ds(col, width))
            pairs = [(ro.at[c], ro_out.at[c])]
        else:
            pairs = [(ri.at[i, s], ri_out.at[s, :, i]) for s in range(SEQS)]
        for src, dst in pairs:
            c = pltpu.make_async_copy(src, dst, lsem.at[4 + len(outs)])
            c.start()
            outs.append(c)

    build(t, refs, where, make, write, loaded)

    started, arrived = {}, set()

    def need(name):
        if name in copies and name not in arrived:
            started[name].wait_recv()
            arrived.add(name)

    names = list(t.items)
    assert sorted(ORDER) == list(range(len(names)))
    for name in [names[i] for i in ORDER]:
        _, deps, emit, kind, _, _ = t.items[name]
        for d in deps:
            need(d)
        r = emit()
        if kind == "send":
            started[name] = r
    for name in copies:
        need(name)
    for name in copies:
        started[name].wait_send()
    for c in outs:
        c.wait()


def rotate(acts, grads, bin_, bout):
    V = pltpu.VMEM
    scratch = [
        V((2, 2, RING, RING, HALF, 7168), BF),
        V((7168, 896), BF),
        V((2, 2, 16, 16, 896), F32),
        V((2, RING, RING, 128, 512), BF),
        V((2, 2, 16, 16, 896), BF),
        V((RING, 256, 512), BF), V((128, 512), BF), V((128, 512), BF),
        V((RING, 2, 2, 256, 256), BF),
        V((2, RING, RING, ROWS, 512), BF),
        V((2, RING, ROWS, 256), BF), V((2, RING, ROWS, 256), BF),
        V((2, RING, ROWS, 512), BF), V((2, RING, ROWS, 512), BF),
        V((2, RING, ROWS, 512), F32), V((RING, ROWS, 512), F32),
        V((2, RING, RING, ROWS, 512), F32),
    ]
    scratch += [V((16, 16, 896), F32), V((16, 16, 896), BF), V((16, 16, 896), BF)] * 2
    count = 240
    scratch += [pltpu.SemaphoreType.DMA((count,)), pltpu.SemaphoreType.DMA((count,)), pltpu.SemaphoreType.DMA((16,))]
    any_ = pl.BlockSpec(memory_space=pl.ANY)
    return pl.pallas_call(
        rotate_kernel,
        out_shape=(
            jax.ShapeDtypeStruct((2, 16, 2, 256 // 16, 896), BF),
            jax.ShapeDtypeStruct((2, RING, RING, 128, 512), BF),
        ),
        in_specs=[any_] * 4,
        out_specs=[any_] * 2,
        scratch_shapes=scratch,
        compiler_params=pltpu.CompilerParams(
            collective_id=0, has_side_effects=True, vmem_limit_bytes=67043328),
        name="rotate",
    )(acts, grads, bin_, bout)


def final_kernel(ro_ref, ri_ref, o_ref):
    total = None
    for s in range(SEQS):
        r = lax.dot_general(
            ro_ref[s].reshape(512, -1), ri_ref[pl.ds(s * 512, 512), :],
            (((0,), (0,)), ((), ())), preferred_element_type=F32)
        total = r * r if total is None else total + r * r
    o_ref[...] = total * (1.0 / SEQS)


def final(ro, ri):
    tile = 512
    return pl.pallas_call(
        final_kernel,
        grid=(2048 // tile,),
        in_specs=[
            pl.BlockSpec((2, RING, None, 128, tile), lambda i: (0, 0, i, 0, 0)),
            pl.BlockSpec((1024, 896), lambda i: (0, 0)),
        ],
        out_specs=pl.BlockSpec((tile, 896), lambda i: (i, 0)),
        out_shape=jax.ShapeDtypeStruct((2048, 896), F32),
        name="final",
    )(ro, ri)


def body(activations, out_grads, basis_in, basis_out):
    ri, ro = rotate(activations, out_grads, basis_in, basis_out)
    return final(ro, ri.reshape(1024, 896))


def solution(mesh):
    in_specs = (P("wide", "narrow"), P("narrow", "wide"), P("narrow", "wide"), P("wide", "narrow"))
    return jax.shard_map(body, mesh=mesh, in_specs=in_specs, out_specs=P("narrow", "wide"), check_vma=False)
```

```python
import functools

import jax
import jax.numpy as jnp
from jax import lax
from jax.experimental import pallas as pl
from jax.experimental.pallas import tpu as pltpu
from jax.sharding import PartitionSpec as P

MESH = pl.DeviceIdType.MESH
BF, F32 = jnp.bfloat16, jnp.float32
SEQS = 2
ROWS = 32
HALF = 16
RING = 4
T = 128

PIECES = (
    ((7, "zxy"), (6, "zyx"), (7, "zxy"), (6, "zyx"), (5, "zxy"), (3, "zyx"), (5, "xyz"), (6, "yxz"), (5, "xyz"), (6, "yxz")),
    ((8, "zxy"), (6, "zyx"), (8, "zxy"), (6, "zyx"), (8, "zxy"), (6, "zyx"), (7, "xyz"), (7, "yxz")),
)
OUT_GATHER = ((0, 64, 0, 256, "zxy"), (0, 64, 256, 256, "zyx"), (64, 64, 0, 256, "zyx"), (64, 64, 256, 256, "zxy"),)
ORDER = (
    4, 5, 0, 248, 207, 249, 157, 146, 147, 136, 237, 125, 104, 227, 158, 124, 238, 197, 94, 187, 135, 3, 177, 2, 1, 64, 250, 209,
    208, 251, 74, 159, 138, 217, 160, 229, 114, 228, 8, 137, 95, 96, 188, 189, 211, 210, 126, 127, 84, 149, 66, 239, 76, 75, 148,
    65, 230, 231, 115, 199, 116, 139, 97, 98, 140, 190, 191, 198, 128, 129, 77, 78, 150, 151, 240, 106, 105, 68, 67, 117, 10, 118,
    9, 130, 131, 241, 242, 152, 153, 70, 69, 132, 201, 200, 142, 133, 141, 108, 107, 7, 119, 244, 243, 11, 12, 154, 203, 202, 85,
    86, 143, 161, 179, 134, 120, 110, 121, 109, 6, 13, 246, 162, 72, 87, 88, 71, 218, 181, 253, 205, 163, 204, 252, 155, 122, 14,
    16, 15, 164, 219, 192, 245, 73, 255, 112, 89, 123, 90, 193, 178, 206, 220, 166, 156, 79, 17, 19, 18, 221, 80, 20, 165, 247, 180,
    99, 100, 91, 92, 144, 81, 182, 183, 195, 254, 21, 22, 82, 232, 167, 93, 111, 102, 223, 145, 101, 222, 233, 257, 194, 83, 212,
    213, 185, 113, 23, 103, 184, 44, 24, 168, 34, 234, 196, 54, 225, 256, 235, 224, 169, 46, 45, 26, 25, 214, 215, 36, 35, 186, 56,
    173, 55, 236, 226, 28, 27, 47, 48, 38, 258, 170, 37, 216, 259, 57, 58, 30, 29, 49, 50, 174, 175, 260, 264, 60, 39, 40, 59, 261,
    171, 172, 32, 31, 51, 52, 176, 265, 266, 62, 61, 41, 42, 33, 53, 262, 263, 63, 43, 267,
)


class Tasks:
    def __init__(self):
        self.items = {}

    def add(self, name, deps, emit, kind, link=None, cost=0.0):
        self.items[name] = (name, tuple(deps), emit, kind, link, cost)


def ax_index(axis, where, at, gathered):
    return slice(None) if axis in gathered else at.get(axis, where[axis])


def build(t, refs, where, make, write, loaded):
    bout, abuf, bvm, part, ro, rs, ex, ri = refs
    x, y, z, zh, core = (where[k] for k in ("x", "y", "z", "zh", "core"))

    def nxt(axis, d):
        return lax.rem(where[axis] + (RING + d), RING)

    def gather(tag, buf, dtype_bytes, rows, col, width, order, deps, part_rows=slice(None)):
        gathered = ()
        blocks = 1
        for axis in order:
            def region(at, c, w, gathered=gathered, axis=axis):
                i = tuple(ax_index(a, where, {axis: at}, gathered) for a in "zyx")
                return buf.at[i + (part_rows, pl.ds(c, w))]
            bytes_ = blocks * rows * dtype_bytes
            me = where[axis]
            if axis == "z":
                parts = ((0, width),)
                if blocks > 1:
                    cut = width // T // 2 * T
                    parts = ((0, cut), (cut, width - cut))
                deps_z = []
                for i, (c, w) in enumerate(parts):
                    r = region(me, col + c, w)
                    make(t, tag + "z%d" % i, deps, r, r, "zA", bytes_ * w)
                    deps_z.append(tag + "z%d" % i)
                deps = deps_z
                blocks *= 2
            else:
                first = (width // T + (int(tag[-1]) + 1) % 2) // 2 * T
                pl_, mi = axis + "+", axis + "-"
                a, b, c, d = (tag + axis + k for k in ("p", "m", "fp", "fm"))
                make(t, a, deps, region(me, col, width), region(me, col, width), pl_, bytes_ * width)
                make(t, b, deps, region(me, col, width), region(me, col, width), mi, bytes_ * width)
                left, right = nxt(axis, -1), nxt(axis, 1)
                make(t, c, [a], region(left, col, first), region(left, col, first), pl_, bytes_ * first)
                deps = [a, b, c]
                if width > first:
                    rc, rw = col + first, width - first
                    make(t, d, [b], region(right, rc, rw), region(right, rc, rw), mi, bytes_ * rw)
                    deps = [a, b, c, d]
                blocks *= RING
            gathered = gathered + (axis,)
        return deps

    bo4, bora, borb, g4, qb, t1, t2, u1, u2, r1, z1, qf = rs
    bov = [bout.at[:, pl.ds(pl.multiple_of(lax.rem(x + k, RING) * 512, 512), 512)] for k in range(RING)]
    left, right, far = nxt("x", -1), nxt("x", 1), nxt("x", 2)
    blk = 256 * 512 * 2
    make(t, "bp", [], bov[1], bo4.at[x], "x+", blk)
    make(t, "bm", [], bov[3], bo4.at[x], "x-", blk)
    make(t, "bfp", [], bov[2].at[pl.ds(0, 128)], bora, "x+", blk // 2)
    make(t, "bfm", [], bov[2].at[pl.ds(128, 128)], borb, "x-", blk // 2)
    make(t, "brp", ["bfp"], bora, bo4.at[left, pl.ds(0, 128)], "x+", blk // 2)
    make(t, "brm", ["bfm"], borb, bo4.at[right, pl.ds(128, 128)], "x-", blk // 2)
    gblk = 256 * 256 * 2
    make(t, "gz", ["ld_g"], g4.at[x, zh, core], g4.at[x, zh, core], "z2", gblk)
    mine, both = g4.at[x, :, core], g4.at[:, :, core]
    make(t, "gp", ["gz"], mine, mine, "x+", 2 * gblk)
    make(t, "gm", ["gz"], mine, mine, "x-", 2 * gblk)
    make(t, "gfp", ["gp"], g4.at[left, 0, core], g4.at[left, 0, core], "x+", gblk)
    make(t, "gfm", ["gm"], g4.at[right, 1, core], g4.at[right, 1, core], "x-", gblk)
    make(t, "gc", ["gp", "gm", "gfp", "gfm"], both, both, "core", 8 * gblk)

    def mul_out():
        loaded("bo")

        def step(i, carry):
            a, b = i // 2, i % 2
            v = None
            for k in range(RING):
                d = jnp.dot(g4[k, a, b], bo4[k], preferred_element_type=F32)
                v = d if v is None else v + d
            v = v.reshape(2, RING, ROWS, 512)
            qf[a, pl.ds(b * 2, 2)] = v
            qb[a, pl.ds(b * 2, 2)] = v.astype(BF)
            return carry
        lax.fori_loop(0, 4, step, 0)
    t.add("mo", ["gc", "bp", "bm", "brp", "brm"], mul_out, "compute", cost=3.0)

    left, right, far = nxt("y", -1), nxt("y", 1), nxt("y", 2)
    big = 8 * ROWS * 2
    lo, hi = pl.ds(0, 256), pl.ds(256, 256)
    make(t, "ra", ["mo"], qb.at[:, far, :, :, lo], t1, "y+", big * 256)
    make(t, "rb", ["mo"], qb.at[:, far, :, :, hi], t2, "y-", big * 256)

    def acc(at, c, t_):
        def run():
            qb[:, at, :, :, c] = (qf[:, at, :, :, c] + t_[...].astype(F32)).astype(BF)
        return run
    t.add("raa", ["ra"], acc(right, lo, t1), "compute", cost=0.5)
    make(t, "rc", ["raa"], qb.at[:, right], u1, "y+", big * 512)
    t.add("rbb", ["rb"], acc(left, hi, t2), "compute", cost=0.5)
    make(t, "rd", ["rbb"], qb.at[:, left], u2, "y-", big * 512)

    def sum1():
        r1[...] = qf[:, y] + u1[...].astype(F32) + u2[...].astype(F32)
    t.add("rs", ["rc", "rd"], sum1, "compute", cost=0.8)
    make(t, "rz", ["rs"], r1.at[1 - z], z1, "zA", 128 * 512 * 4)

    def sum2():
        ro[z, y, x] = (r1[z] + z1[...]).astype(BF).reshape(128, 512)
    t.add("rt", ["rz"], sum2, "compute", cost=0.4)
    for p, (row, rows, col, width, order) in enumerate(OUT_GATHER):
        deps = gather("o%d" % p, ro, 2, rows, col, width, order, ["rt"], pl.ds(row, rows))
        t.add("v%d" % p, deps, lambda p=p: write("ro", p), "compute", cost=0.1)

    begun = set()
    for h in range(2):
        ab = abuf.at[h]
        col, muls = 0, []
        for j, (tiles, order) in enumerate(PIECES[h]):
            width = tiles * T
            tag = "a%d%d" % (h, j)
            deps = gather(tag, ab, 2, HALF, col, width, order, ["ld_a"])

            def mul(col=col, width=width, h=h):
                loaded("b")
                first = h not in begun
                begun.add(h)

                def step(s, carry):
                    v = jnp.dot(
                        abuf[h, s, :, :, :, pl.ds(col, width)].reshape(256, width),
                        bvm[pl.ds(col, width), :],
                        preferred_element_type=F32,
                    ).reshape(16, 16, 896)
                    if first:
                        part[h, s] = v
                    else:
                        part[h, s] += v
                    return carry
                lax.fori_loop(0, 2, step, 0)
            t.add(tag + "mul", deps, mul, "compute", cost=tiles * 0.17)
            muls.append(tag + "mul")
            col += width
        k = "e%d" % h
        wide_, thin = 8 * 16 * 896 * 4, 8 * 16 * 896 * 2

        e1, eb, er = ex[h]
        make(t, k + "x", muls, part.at[h, 1 - core], e1, "core", 2 * wide_)

        def add1(h=h, e1=e1, eb=eb):
            v = part[h, core] + e1[...]
            part[h, core] = v
            eb[...] = v.astype(BF)
        t.add(k + "s", [k + "x"], add1, "compute", cost=0.5)
        done = []
        for i in range(2):
            c, rows = k + str(i), pl.ds(i * 8, 8)
            make(t, c + "a", [k + "s"], eb.at[rows], er.at[rows], "z2", thin)

            def add2(h=h, er=er, rows=rows):
                ri[h, core, rows] = (part[h, core, rows] + er[rows].astype(F32)).astype(BF)
            t.add(c + "t", [c + "a"], add2, "compute", cost=0.2)
            mine = ri.at[h, core, rows]
            make(t, c + "f", [c + "t"], mine, mine, "core", thin)
            done += [c + "t", c + "f"]
        t.add("w%d" % h, done, lambda h=h: write("ri", h), "compute", cost=0.1)
    return


def rotate_kernel(acts, grads, bin_, bout, ri_out, ro_out, *scratch):
    (abuf, bvm, part, ro, ri), rest = scratch[:5], scratch[5:]
    rs = rest[0:12]
    ex = [rest[12:15], rest[15:18]]
    ssem, rsem, lsem = rest[18:]
    bo4, g4 = rs[0], rs[3]
    w, n = lax.axis_index("wide"), lax.axis_index("narrow")
    z, y, x = w // 16, (w // 4) % 4, w % 4
    zh, core = n // 2, n % 2
    where = dict(x=x, y=y, z=z, zh=zh, core=core)

    def dev(z_, y_, x_, zh_, core_):
        return {"wide": z_ * 16 + y_ * 4 + x_, "narrow": zh_ * 2 + core_}

    ring = lambda v, d: lax.rem(v + (RING + d), RING)
    peers = {
        "x+": dev(z, y, ring(x, 1), zh, core),
        "x-": dev(z, y, ring(x, -1), zh, core),
        "y+": dev(z, ring(y, 1), x, zh, core),
        "y-": dev(z, ring(y, -1), x, zh, core),
        "zA": dev(1 - z, y, x, zh, core),
        "z2": dev(z, y, x, 1 - zh, core),
        "core": dev(z, y, x, zh, 1 - core),
    }

    local = {}

    def load(name, src, dst):
        c = pltpu.make_async_copy(src, dst, lsem.at[len(local)])
        c.start()
        local[name] = c

    for h in range(2):
        load("a%d" % h, acts.at[pl.ds(h * HALF, HALF)], abuf.at[h, z, y, x])
    load("g", grads, g4.at[x, zh, core])
    load("bo", bout.at[:, pl.ds(pl.multiple_of(x * 512, 512), 512)], bo4.at[x])
    barrier = pltpu.get_barrier_semaphore()
    for p in peers.values():
        pl.semaphore_signal(barrier, inc=1, device_id=p, device_id_type=MESH)
    pl.semaphore_wait(barrier, len(peers))
    load("b", bin_, bvm)

    t = Tasks()
    copies = {}

    def make(t, name, deps, src, dst, link, nbytes):
        i = len(copies)
        copies[name] = (i, src, dst, link)

        def emit():
            d = pltpu.make_async_remote_copy(
                src_ref=src, dst_ref=dst, send_sem=ssem.at[i], recv_sem=rsem.at[i],
                device_id=peers[link], device_id_type=MESH)
            d.start()
            return d
        t.add(name, deps, emit, "send", link, nbytes)

    def loaded(*names):
        for name in names:
            if name in local:
                local.pop(name).wait()

    t.add("ld_a", [], lambda: loaded("a0", "a1"), "compute", cost=0.5)
    t.add("ld_g", [], lambda: loaded("g"), "compute", cost=0.3)

    refs = (bout, abuf, bvm, part, ro, rs, ex, ri)
    outs = []

    def write(what, i):
        if what == "ro":
            row, rows, col, width, _ = OUT_GATHER[i]
            c = (slice(None),) * 3 + (pl.ds(row, rows), pl.ds(col, width))
            pairs = [(ro.at[c], ro_out.at[c])]
        else:
            pairs = [(ri.at[i, s], ri_out.at[s, :, i]) for s in range(SEQS)]
        for src, dst in pairs:
            c = pltpu.make_async_copy(src, dst, lsem.at[4 + len(outs)])
            c.start()
            outs.append(c)

    build(t, refs, where, make, write, loaded)

    started, arrived = {}, set()

    def need(name):
        if name in copies and name not in arrived:
            started[name].wait_recv()
            arrived.add(name)

    names = list(t.items)
    assert sorted(ORDER) == list(range(len(names)))
    for name in [names[i] for i in ORDER]:
        _, deps, emit, kind, _, _ = t.items[name]
        for d in deps:
            need(d)
        r = emit()
        if kind == "send":
            started[name] = r
    for name in copies:
        need(name)
    for name in copies:
        started[name].wait_send()
    for c in outs:
        c.wait()


def rotate(acts, grads, bin_, bout):
    V = pltpu.VMEM
    scratch = [
        V((2, 2, RING, RING, HALF, 7168), BF),
        V((7168, 896), BF),
        V((2, 2, 16, 16, 896), F32),
        V((2, RING, RING, 128, 512), BF),
        V((2, 2, 16, 16, 896), BF),
        V((RING, 256, 512), BF), V((128, 512), BF), V((128, 512), BF),
        V((RING, 2, 2, 256, 256), BF),
        V((2, RING, RING, ROWS, 512), BF),
        V((2, RING, ROWS, 256), BF), V((2, RING, ROWS, 256), BF),
        V((2, RING, ROWS, 512), BF), V((2, RING, ROWS, 512), BF),
        V((2, RING, ROWS, 512), F32), V((RING, ROWS, 512), F32),
        V((2, RING, RING, ROWS, 512), F32),
    ]
    scratch += [V((16, 16, 896), F32), V((16, 16, 896), BF), V((16, 16, 896), BF)] * 2
    count = 240
    scratch += [pltpu.SemaphoreType.DMA((count,)), pltpu.SemaphoreType.DMA((count,)), pltpu.SemaphoreType.DMA((16,))]
    any_ = pl.BlockSpec(memory_space=pl.ANY)
    return pl.pallas_call(
        rotate_kernel,
        out_shape=(
            jax.ShapeDtypeStruct((2, 16, 2, 256 // 16, 896), BF),
            jax.ShapeDtypeStruct((2, RING, RING, 128, 512), BF),
        ),
        in_specs=[any_] * 4,
        out_specs=[any_] * 2,
        scratch_shapes=scratch,
        compiler_params=pltpu.CompilerParams(
            collective_id=0, has_side_effects=True, vmem_limit_bytes=67043328),
        name="rotate",
    )(acts, grads, bin_, bout)


def final_kernel(ro_ref, ri_ref, o_ref):
    total = None
    for s in range(SEQS):
        r = lax.dot_general(
            ro_ref[s].reshape(512, -1), ri_ref[pl.ds(s * 512, 512), :],
            (((0,), (0,)), ((), ())), preferred_element_type=F32)
        total = r * r if total is None else total + r * r
    o_ref[...] = total * (1.0 / SEQS)


def final(ro, ri):
    tile = 512
    return pl.pallas_call(
        final_kernel,
        grid=(2048 // tile,),
        in_specs=[
            pl.BlockSpec((2, RING, None, 128, tile), lambda i: (0, 0, i, 0, 0)),
            pl.BlockSpec((1024, 896), lambda i: (0, 0)),
        ],
        out_specs=pl.BlockSpec((tile, 896), lambda i: (i, 0)),
        out_shape=jax.ShapeDtypeStruct((2048, 896), F32),
        name="final",
    )(ro, ri)


def body(activations, out_grads, basis_in, basis_out):
    ri, ro = rotate(activations, out_grads, basis_in, basis_out)
    return final(ro, ri.reshape(1024, 896))


def solution(mesh):
    in_specs = (P("wide", "narrow"), P("narrow", "wide"), P("narrow", "wide"), P("wide", "narrow"))
    return jax.shard_map(body, mesh=mesh, in_specs=in_specs, out_specs=P("narrow", "wide"), check_vma=False)
```

```python
import functools

import jax
import jax.numpy as jnp
from jax import lax
from jax.experimental import pallas as pl
from jax.experimental.pallas import tpu as pltpu
from jax.sharding import PartitionSpec as P

MESH = pl.DeviceIdType.MESH
BF, F32 = jnp.bfloat16, jnp.float32
SEQS = 2
ROWS = 32
HALF = 16
RING = 4
T = 128

PIECES = (
    ((7, "zxy"), (6, "zyx"), (7, "zxy"), (6, "zyx"), (5, "zxy"), (3, "zyx"), (5, "xyz"), (6, "yxz"), (5, "xyz"), (6, "yxz")),
    ((8, "zxy"), (6, "zyx"), (8, "zxy"), (6, "zyx"), (8, "zxy"), (6, "zyx"), (7, "xyz"), (7, "yxz")),
)
OUT_GATHER = ((0, 64, 0, 256, "zxy"), (0, 64, 256, 256, "zyx"), (64, 64, 0, 256, "zyx"), (64, 64, 256, 256, "zxy"),)
ORDER = (
    4, 5, 0, 248, 207, 249, 157, 146, 147, 136, 237, 125, 104, 227, 158, 124, 238, 197, 94, 187, 135, 3, 177, 2, 1, 64, 250, 209,
    208, 251, 74, 159, 138, 217, 160, 229, 114, 228, 8, 137, 95, 96, 188, 189, 211, 210, 126, 127, 84, 149, 66, 239, 76, 75, 148,
    65, 230, 231, 115, 199, 116, 139, 97, 98, 140, 190, 191, 198, 128, 129, 77, 78, 150, 151, 240, 106, 105, 68, 67, 117, 10, 118,
    9, 130, 131, 241, 242, 152, 153, 70, 69, 132, 201, 200, 142, 133, 141, 108, 107, 7, 119, 244, 243, 11, 12, 154, 203, 202, 85,
    86, 143, 161, 179, 134, 120, 110, 121, 109, 6, 13, 246, 162, 72, 87, 88, 71, 218, 181, 253, 205, 163, 204, 252, 155, 122, 14,
    16, 15, 164, 219, 192, 245, 73, 255, 112, 89, 123, 90, 193, 178, 206, 220, 166, 156, 79, 17, 19, 18, 221, 80, 20, 165, 247, 180,
    99, 100, 91, 92, 144, 81, 182, 183, 195, 254, 21, 22, 82, 232, 167, 93, 111, 102, 223, 145, 101, 222, 233, 257, 194, 83, 212,
    213, 185, 113, 23, 103, 184, 44, 24, 168, 34, 234, 196, 54, 225, 256, 235, 224, 169, 46, 45, 26, 25, 214, 215, 36, 35, 186, 56,
    173, 55, 236, 226, 28, 27, 47, 48, 38, 258, 170, 37, 216, 259, 57, 58, 30, 29, 49, 50, 174, 175, 260, 264, 60, 39, 40, 59, 261,
    171, 172, 32, 31, 51, 52, 176, 265, 266, 62, 61, 41, 42, 33, 53, 262, 263, 63, 43, 267,
)


class Tasks:
    def __init__(self):
        self.items = {}

    def add(self, name, deps, emit, kind, link=None, cost=0.0):
        self.items[name] = (name, tuple(deps), emit, kind, link, cost)


def ax_index(axis, where, at, gathered):
    return slice(None) if axis in gathered else at.get(axis, where[axis])


def build(t, refs, where, make, write, loaded):
    bout, abuf, bvm, part, ro, rs, ex, ri = refs
    x, y, z, zh, core = (where[k] for k in ("x", "y", "z", "zh", "core"))

    def nxt(axis, d):
        return lax.rem(where[axis] + (RING + d), RING)

    def gather(tag, buf, dtype_bytes, rows, col, width, order, deps, part_rows=slice(None)):
        gathered = ()
        blocks = 1
        for axis in order:
            def region(at, c, w, gathered=gathered, axis=axis):
                i = tuple(ax_index(a, where, {axis: at}, gathered) for a in "zyx")
                return buf.at[i + (part_rows, pl.ds(c, w))]
            bytes_ = blocks * rows * dtype_bytes
            me = where[axis]
            if axis == "z":
                parts = ((0, width),)
                if blocks > 1:
                    cut = width // T // 2 * T
                    parts = ((0, cut), (cut, width - cut))
                deps_z = []
                for i, (c, w) in enumerate(parts):
                    r = region(me, col + c, w)
                    make(t, tag + "z%d" % i, deps, r, r, "zA", bytes_ * w)
                    deps_z.append(tag + "z%d" % i)
                deps = deps_z
                blocks *= 2
            else:
                first = (width // T + (int(tag[-1]) + 1) % 2) // 2 * T
                pl_, mi = axis + "+", axis + "-"
                a, b, c, d = (tag + axis + k for k in ("p", "m", "fp", "fm"))
                make(t, a, deps, region(me, col, width), region(me, col, width), pl_, bytes_ * width)
                make(t, b, deps, region(me, col, width), region(me, col, width), mi, bytes_ * width)
                left, right = nxt(axis, -1), nxt(axis, 1)
                make(t, c, [a], region(left, col, first), region(left, col, first), pl_, bytes_ * first)
                deps = [a, b, c]
                if width > first:
                    rc, rw = col + first, width - first
                    make(t, d, [b], region(right, rc, rw), region(right, rc, rw), mi, bytes_ * rw)
                    deps = [a, b, c, d]
                blocks *= RING
            gathered = gathered + (axis,)
        return deps

    bo4, bora, borb, g4, qb, t1, t2, u1, u2, r1, z1, qf = rs
    bov = [bout.at[:, pl.ds(pl.multiple_of(lax.rem(x + k, RING) * 512, 512), 512)] for k in range(RING)]
    left, right, far = nxt("x", -1), nxt("x", 1), nxt("x", 2)
    blk = 256 * 512 * 2
    make(t, "bp", [], bov[1], bo4.at[x], "x+", blk)
    make(t, "bm", [], bov[3], bo4.at[x], "x-", blk)
    make(t, "bfp", [], bov[2].at[pl.ds(0, 128)], bora, "x+", blk // 2)
    make(t, "bfm", [], bov[2].at[pl.ds(128, 128)], borb, "x-", blk // 2)
    make(t, "brp", ["bfp"], bora, bo4.at[left, pl.ds(0, 128)], "x+", blk // 2)
    make(t, "brm", ["bfm"], borb, bo4.at[right, pl.ds(128, 128)], "x-", blk // 2)
    gblk = 256 * 256 * 2
    make(t, "gz", ["ld_g"], g4.at[x, zh, core], g4.at[x, zh, core], "z2", gblk)
    mine, both = g4.at[x, :, core], g4.at[:, :, core]
    make(t, "gp", ["gz"], mine, mine, "x+", 2 * gblk)
    make(t, "gm", ["gz"], mine, mine, "x-", 2 * gblk)
    make(t, "gfp", ["gp"], g4.at[left, 0, core], g4.at[left, 0, core], "x+", gblk)
    make(t, "gfm", ["gm"], g4.at[right, 1, core], g4.at[right, 1, core], "x-", gblk)
    make(t, "gc", ["gp", "gm", "gfp", "gfm"], both, both, "core", 8 * gblk)

    def mul_out():
        loaded("bo")

        def step(i, carry):
            a, b = i // 2, i % 2
            v = None
            for k in range(RING):
                d = jnp.dot(g4[k, a, b], bo4[k], preferred_element_type=F32)
                v = d if v is None else v + d
            v = v.reshape(2, RING, ROWS, 512)
            qf[a, pl.ds(b * 2, 2)] = v
            qb[a, pl.ds(b * 2, 2)] = v.astype(BF)
            return carry
        lax.fori_loop(0, 4, step, 0)
    t.add("mo", ["gc", "bp", "bm", "brp", "brm"], mul_out, "compute", cost=3.0)

    left, right, far = nxt("y", -1), nxt("y", 1), nxt("y", 2)
    big = 8 * ROWS * 2
    lo, hi = pl.ds(0, 256), pl.ds(256, 256)
    make(t, "ra", ["mo"], qb.at[:, far, :, :, lo], t1, "y+", big * 256)
    make(t, "rb", ["mo"], qb.at[:, far, :, :, hi], t2, "y-", big * 256)

    def acc(at, c, t_):
        def run():
            qb[:, at, :, :, c] = (qf[:, at, :, :, c] + t_[...].astype(F32)).astype(BF)
        return run
    t.add("raa", ["ra"], acc(right, lo, t1), "compute", cost=0.5)
    make(t, "rc", ["raa"], qb.at[:, right], u1, "y+", big * 512)
    t.add("rbb", ["rb"], acc(left, hi, t2), "compute", cost=0.5)
    make(t, "rd", ["rbb"], qb.at[:, left], u2, "y-", big * 512)

    def sum1():
        r1[...] = qf[:, y] + u1[...].astype(F32) + u2[...].astype(F32)
    t.add("rs", ["rc", "rd"], sum1, "compute", cost=0.8)
    make(t, "rz", ["rs"], r1.at[1 - z], z1, "zA", 128 * 512 * 4)

    def sum2():
        ro[z, y, x] = (r1[z] + z1[...]).astype(BF).reshape(128, 512)
    t.add("rt", ["rz"], sum2, "compute", cost=0.4)
    for p, (row, rows, col, width, order) in enumerate(OUT_GATHER):
        deps = gather("o%d" % p, ro, 2, rows, col, width, order, ["rt"], pl.ds(row, rows))
        t.add("v%d" % p, deps, lambda p=p: write("ro", p), "compute", cost=0.1)

    begun = set()
    for h in range(2):
        ab = abuf.at[h]
        col, muls = 0, []
        for j, (tiles, order) in enumerate(PIECES[h]):
            width = tiles * T
            tag = "a%d%d" % (h, j)
            deps = gather(tag, ab, 2, HALF, col, width, order, ["ld_a"])

            def mul(col=col, width=width, h=h):
                loaded("b")
                first = h not in begun
                begun.add(h)

                def step(s, carry):
                    v = jnp.dot(
                        abuf[h, s, :, :, :, pl.ds(col, width)].reshape(256, width),
                        bvm[pl.ds(col, width), :],
                        preferred_element_type=F32,
                    ).reshape(16, 16, 896)
                    if first:
                        part[h, s] = v
                    else:
                        part[h, s] += v
                    return carry
                lax.fori_loop(0, 2, step, 0)
            t.add(tag + "mul", deps, mul, "compute", cost=tiles * 0.17)
            muls.append(tag + "mul")
            col += width
        k = "e%d" % h
        wide_, thin = 8 * 16 * 896 * 4, 8 * 16 * 896 * 2

        e1, eb, er = ex[h]
        make(t, k + "x", muls, part.at[h, 1 - core], e1, "core", 2 * wide_)

        def add1(h=h, e1=e1, eb=eb):
            v = part[h, core] + e1[...]
            part[h, core] = v
            eb[...] = v.astype(BF)
        t.add(k + "s", [k + "x"], add1, "compute", cost=0.5)
        done = []
        for i in range(2):
            c, rows = k + str(i), pl.ds(i * 8, 8)
            make(t, c + "a", [k + "s"], eb.at[rows], er.at[rows], "z2", thin)

            def add2(h=h, er=er, rows=rows):
                ri[h, core, rows] = (part[h, core, rows] + er[rows].astype(F32)).astype(BF)
            t.add(c + "t", [c + "a"], add2, "compute", cost=0.2)
            mine = ri.at[h, core, rows]
            make(t, c + "f", [c + "t"], mine, mine, "core", thin)
            done += [c + "t", c + "f"]
        t.add("w%d" % h, done, lambda h=h: write("ri", h), "compute", cost=0.1)
    return


def rotate_kernel(acts, grads, bin_, bout, ri_out, ro_out, *scratch):
    (abuf, bvm, part, ro, ri), rest = scratch[:5], scratch[5:]
    rs = rest[0:12]
    ex = [rest[12:15], rest[15:18]]
    ssem, rsem, lsem = rest[18:]
    bo4, g4 = rs[0], rs[3]
    w, n = lax.axis_index("wide"), lax.axis_index("narrow")
    z, y, x = w // 16, (w // 4) % 4, w % 4
    zh, core = n // 2, n % 2
    where = dict(x=x, y=y, z=z, zh=zh, core=core)

    def dev(z_, y_, x_, zh_, core_):
        return {"wide": z_ * 16 + y_ * 4 + x_, "narrow": zh_ * 2 + core_}

    ring = lambda v, d: lax.rem(v + (RING + d), RING)
    peers = {
        "x+": dev(z, y, ring(x, 1), zh, core),
        "x-": dev(z, y, ring(x, -1), zh, core),
        "y+": dev(z, ring(y, 1), x, zh, core),
        "y-": dev(z, ring(y, -1), x, zh, core),
        "zA": dev(1 - z, y, x, zh, core),
        "z2": dev(z, y, x, 1 - zh, core),
        "core": dev(z, y, x, zh, 1 - core),
    }

    local = {}

    def load(name, src, dst):
        c = pltpu.make_async_copy(src, dst, lsem.at[len(local)])
        c.start()
        local[name] = c

    for h in range(2):
        load("a%d" % h, acts.at[pl.ds(h * HALF, HALF)], abuf.at[h, z, y, x])
    load("g", grads, g4.at[x, zh, core])
    load("bo", bout.at[:, pl.ds(pl.multiple_of(x * 512, 512), 512)], bo4.at[x])
    barrier = pltpu.get_barrier_semaphore()
    for p in peers.values():
        pl.semaphore_signal(barrier, inc=1, device_id=p, device_id_type=MESH)
    pl.semaphore_wait(barrier, len(peers))
    load("b", bin_, bvm)

    t = Tasks()
    copies = {}

    def make(t, name, deps, src, dst, link, nbytes):
        i = len(copies)
        copies[name] = (i, src, dst, link)

        def emit():
            d = pltpu.make_async_remote_copy(
                src_ref=src, dst_ref=dst, send_sem=ssem.at[i], recv_sem=rsem.at[i],
                device_id=peers[link], device_id_type=MESH)
            d.start()
            return d
        t.add(name, deps, emit, "send", link, nbytes)

    def loaded(*names):
        for name in names:
            if name in local:
                local.pop(name).wait()

    t.add("ld_a", [], lambda: loaded("a0", "a1"), "compute", cost=0.5)
    t.add("ld_g", [], lambda: loaded("g"), "compute", cost=0.3)

    refs = (bout, abuf, bvm, part, ro, rs, ex, ri)
    outs = []

    def write(what, i):
        if what == "ro":
            row, rows, col, width, _ = OUT_GATHER[i]
            c = (slice(None),) * 3 + (pl.ds(row, rows), pl.ds(col, width))
            pairs = [(ro.at[c], ro_out.at[c])]
        else:
            pairs = [(ri.at[i, s], ri_out.at[s, :, i]) for s in range(SEQS)]
        for src, dst in pairs:
            c = pltpu.make_async_copy(src, dst, lsem.at[4 + len(outs)])
            c.start()
            outs.append(c)

    build(t, refs, where, make, write, loaded)

    started, arrived = {}, set()

    def need(name):
        if name in copies and name not in arrived:
            started[name].wait_recv()
            arrived.add(name)

    names = list(t.items)
    assert sorted(ORDER) == list(range(len(names)))
    for name in [names[i] for i in ORDER]:
        _, deps, emit, kind, _, _ = t.items[name]
        for d in deps:
            need(d)
        r = emit()
        if kind == "send":
            started[name] = r
    for name in copies:
        need(name)
    for name in copies:
        started[name].wait_send()
    for c in outs:
        c.wait()


def rotate(acts, grads, bin_, bout):
    V = pltpu.VMEM
    scratch = [
        V((2, 2, RING, RING, HALF, 7168), BF),
        V((7168, 896), BF),
        V((2, 2, 16, 16, 896), F32),
        V((2, RING, RING, 128, 512), BF),
        V((2, 2, 16, 16, 896), BF),
        V((RING, 256, 512), BF), V((128, 512), BF), V((128, 512), BF),
        V((RING, 2, 2, 256, 256), BF),
        V((2, RING, RING, ROWS, 512), BF),
        V((2, RING, ROWS, 256), BF), V((2, RING, ROWS, 256), BF),
        V((2, RING, ROWS, 512), BF), V((2, RING, ROWS, 512), BF),
        V((2, RING, ROWS, 512), F32), V((RING, ROWS, 512), F32),
        V((2, RING, RING, ROWS, 512), F32),
    ]
    scratch += [V((16, 16, 896), F32), V((16, 16, 896), BF), V((16, 16, 896), BF)] * 2
    count = 240
    scratch += [pltpu.SemaphoreType.DMA((count,)), pltpu.SemaphoreType.DMA((count,)), pltpu.SemaphoreType.DMA((16,))]
    any_ = pl.BlockSpec(memory_space=pl.ANY)
    return pl.pallas_call(
        rotate_kernel,
        out_shape=(
            jax.ShapeDtypeStruct((2, 16, 2, 256 // 16, 896), BF),
            jax.ShapeDtypeStruct((2, RING, RING, 128, 512), BF),
        ),
        in_specs=[any_] * 4,
        out_specs=[any_] * 2,
        scratch_shapes=scratch,
        compiler_params=pltpu.CompilerParams(
            collective_id=0, has_side_effects=True, vmem_limit_bytes=67043328),
        name="rotate",
    )(acts, grads, bin_, bout)


COLS = ((0, 512), (512, 384))


def final_kernel(ro_any, ri_any, o_any, rov, riv, ov, rsem, isem, osem):
    gets, rows = {}, {}
    for m in range(2):
        for s in range(SEQS):
            gets[m, s] = pltpu.make_async_copy(ro_any.at[s, :, pl.ds(2 * m, 2)], rov.at[m, s], rsem.at[m, s])
            gets[m, s].start()
            if m == 0:
                rows[s] = pltpu.make_async_copy(ri_any.at[pl.ds(s * 512, 512)], riv.at[s], isem.at[s])
                rows[s].start()
    puts = []
    for m in range(2):
        for p, (col, width) in enumerate(COLS):
            total = None
            for s in range(SEQS):
                if p == 0:
                    gets[m, s].wait()
                    if m == 0:
                        rows[s].wait()
                g = jnp.concatenate([rov[m, s, :, b].reshape(512, 512) for b in range(2)], axis=1)
                r = lax.dot_general(
                    g, riv[s, :, pl.ds(col, width)], (((0,), (0,)), ((), ())), preferred_element_type=F32)
                total = r * r if total is None else total + r * r
            ov[m, :, pl.ds(col, width)] = total * (1.0 / SEQS)
            part = pltpu.make_async_copy(
                ov.at[m, :, pl.ds(col, width)], o_any.at[pl.ds(m * 1024, 1024), pl.ds(col, width)], osem.at[m, p])
            part.start()
            puts.append(part)
    for part in puts:
        part.wait()


def final(ro, ri):
    any_ = pl.BlockSpec(memory_space=pl.ANY)
    return pl.pallas_call(
        final_kernel,
        in_specs=[any_, any_],
        out_specs=any_,
        out_shape=jax.ShapeDtypeStruct((2048, 896), F32),
        scratch_shapes=[
            pltpu.VMEM((2, SEQS, RING, 2, 128, 512), BF),
            pltpu.VMEM((SEQS, 512, 896), BF),
            pltpu.VMEM((2, 1024, 896), F32),
            pltpu.SemaphoreType.DMA((2, SEQS)),
            pltpu.SemaphoreType.DMA((SEQS,)),
            pltpu.SemaphoreType.DMA((2, 2)),
        ],
        name="final",
    )(ro, ri)


def body(activations, out_grads, basis_in, basis_out):
    ri, ro = rotate(activations, out_grads, basis_in, basis_out)
    return final(ro, ri.reshape(1024, 896))


def solution(mesh):
    in_specs = (P("wide", "narrow"), P("narrow", "wide"), P("narrow", "wide"), P("wide", "narrow"))
    return jax.shard_map(body, mesh=mesh, in_specs=in_specs, out_specs=P("narrow", "wide"), check_vma=False)
```

```python
import functools

import jax
import jax.numpy as jnp
from jax import lax
from jax.experimental import pallas as pl
from jax.experimental.pallas import tpu as pltpu
from jax.sharding import PartitionSpec as P

MESH = pl.DeviceIdType.MESH
BF, F32 = jnp.bfloat16, jnp.float32
SEQS = 2
ROWS = 32
HALF = 16
RING = 4
T = 128

PIECES = (
    ((7, "zxy"), (6, "zyx"), (7, "zxy"), (6, "zyx"), (5, "zxy"), (3, "zyx"), (5, "xyz"), (6, "yxz"), (5, "xyz"), (6, "yxz")),
    ((8, "zxy"), (6, "zyx"), (8, "zxy"), (6, "zyx"), (8, "zxy"), (6, "zyx"), (7, "xyz"), (7, "yxz")),
)
OUT_GATHER = ((0, 64, 0, 256, "zxy"), (0, 64, 256, 256, "zyx"), (64, 64, 0, 256, "zyx"), (64, 64, 256, 256, "zxy"),)
ORDER = (
    4, 5, 0, 135, 124, 94, 249, 125, 136, 248, 227, 147, 237, 74, 238, 177, 146, 207, 3, 84, 2, 158, 64, 187, 157, 1, 8, 137, 96, 95,
    251, 250, 228, 138, 229, 76, 75, 160, 159, 114, 208, 197, 209, 104, 98, 97, 217, 126, 127, 66, 148, 65, 189, 188, 230, 231,
    240, 239, 7, 85, 77, 78, 139, 115, 116, 210, 211, 149, 86, 128, 129, 190, 191, 218, 219, 241, 242, 67, 68, 9, 117, 118, 10, 130,
    131, 150, 151, 243, 244, 69, 70, 220, 132, 88, 87, 221, 133, 141, 140, 161, 153, 179, 152, 11, 106, 245, 89, 12, 90, 6, 142, 72,
    154, 71, 134, 163, 199, 223, 79, 162, 155, 222, 13, 80, 105, 99, 144, 92, 73, 91, 100, 14, 15, 16, 107, 198, 143, 108, 164, 156,
    181, 252, 225, 224, 201, 120, 246, 178, 93, 101, 109, 110, 102, 19, 17, 20, 82, 200, 192, 145, 18, 166, 253, 226, 180, 122,
    103, 112, 254, 193, 165, 247, 111, 119, 203, 212, 202, 255, 21, 22, 213, 183, 81, 113, 182, 167, 121, 194, 195, 257, 232, 233,
    205, 83, 204, 23, 123, 168, 54, 214, 215, 24, 196, 34, 44, 185, 256, 184, 169, 234, 235, 56, 55, 206, 25, 36, 35, 45, 46, 26,
    173, 216, 186, 236, 58, 57, 38, 37, 170, 27, 258, 259, 28, 48, 47, 59, 60, 39, 40, 260, 264, 174, 175, 29, 30, 49, 50, 261, 171,
    172, 61, 62, 41, 42, 176, 265, 266, 31, 32, 51, 52, 63, 43, 262, 263, 33, 53, 267,
)


class Tasks:
    def __init__(self):
        self.items = {}

    def add(self, name, deps, emit, kind, link=None, cost=0.0):
        self.items[name] = (name, tuple(deps), emit, kind, link, cost)


def ax_index(axis, where, at, gathered):
    return slice(None) if axis in gathered else at.get(axis, where[axis])


def build(t, refs, where, make, write, loaded):
    bout, abuf, bvm, part, ro, rs, ex, ri = refs
    x, y, z, zh, core = (where[k] for k in ("x", "y", "z", "zh", "core"))

    def nxt(axis, d):
        return lax.rem(where[axis] + (RING + d), RING)

    def gather(tag, buf, dtype_bytes, rows, col, width, order, deps, part_rows=slice(None)):
        gathered = ()
        blocks = 1
        for axis in order:
            def region(at, c, w, gathered=gathered, axis=axis):
                i = tuple(ax_index(a, where, {axis: at}, gathered) for a in "zyx")
                return buf.at[i + (part_rows, pl.ds(c, w))]
            bytes_ = blocks * rows * dtype_bytes
            me = where[axis]
            if axis == "z":
                parts = ((0, width),)
                if blocks > 1:
                    cut = width // T // 2 * T
                    parts = ((0, cut), (cut, width - cut))
                deps_z = []
                for i, (c, w) in enumerate(parts):
                    r = region(me, col + c, w)
                    make(t, tag + "z%d" % i, deps, r, r, "zA", bytes_ * w)
                    deps_z.append(tag + "z%d" % i)
                deps = deps_z
                blocks *= 2
            else:
                first = (width // T + (int(tag[-1]) + 1) % 2) // 2 * T
                pl_, mi = axis + "+", axis + "-"
                a, b, c, d = (tag + axis + k for k in ("p", "m", "fp", "fm"))
                make(t, a, deps, region(me, col, width), region(me, col, width), pl_, bytes_ * width)
                make(t, b, deps, region(me, col, width), region(me, col, width), mi, bytes_ * width)
                left, right = nxt(axis, -1), nxt(axis, 1)
                make(t, c, [a], region(left, col, first), region(left, col, first), pl_, bytes_ * first)
                deps = [a, b, c]
                if width > first:
                    rc, rw = col + first, width - first
                    make(t, d, [b], region(right, rc, rw), region(right, rc, rw), mi, bytes_ * rw)
                    deps = [a, b, c, d]
                blocks *= RING
            gathered = gathered + (axis,)
        return deps

    bo4, bora, borb, g4, qb, t1, t2, u1, u2, r1, z1, qf = rs
    bov = [bout.at[:, pl.ds(pl.multiple_of(lax.rem(x + k, RING) * 512, 512), 512)] for k in range(RING)]
    left, right, far = nxt("x", -1), nxt("x", 1), nxt("x", 2)
    blk = 256 * 512 * 2
    make(t, "bp", [], bov[1], bo4.at[x], "x+", blk)
    make(t, "bm", [], bov[3], bo4.at[x], "x-", blk)
    make(t, "bfp", [], bov[2].at[pl.ds(0, 128)], bora, "x+", blk // 2)
    make(t, "bfm", [], bov[2].at[pl.ds(128, 128)], borb, "x-", blk // 2)
    make(t, "brp", ["bfp"], bora, bo4.at[left, pl.ds(0, 128)], "x+", blk // 2)
    make(t, "brm", ["bfm"], borb, bo4.at[right, pl.ds(128, 128)], "x-", blk // 2)
    gblk = 256 * 256 * 2
    make(t, "gz", ["ld_g"], g4.at[x, zh, core], g4.at[x, zh, core], "z2", gblk)
    mine, both = g4.at[x, :, core], g4.at[:, :, core]
    make(t, "gp", ["gz"], mine, mine, "x+", 2 * gblk)
    make(t, "gm", ["gz"], mine, mine, "x-", 2 * gblk)
    make(t, "gfp", ["gp"], g4.at[left, 0, core], g4.at[left, 0, core], "x+", gblk)
    make(t, "gfm", ["gm"], g4.at[right, 1, core], g4.at[right, 1, core], "x-", gblk)
    make(t, "gc", ["gp", "gm", "gfp", "gfm"], both, both, "core", 8 * gblk)

    def mul_out():
        loaded("bo")

        def step(i, carry):
            a, b = i // 2, i % 2
            v = None
            for k in range(RING):
                d = jnp.dot(g4[k, a, b], bo4[k], preferred_element_type=F32)
                v = d if v is None else v + d
            v = v.reshape(2, RING, ROWS, 512)
            qf[a, pl.ds(b * 2, 2)] = v
            qb[a, pl.ds(b * 2, 2)] = v.astype(BF)
            return carry
        lax.fori_loop(0, 4, step, 0)
    t.add("mo", ["gc", "bp", "bm", "brp", "brm"], mul_out, "compute", cost=3.0)

    left, right, far = nxt("y", -1), nxt("y", 1), nxt("y", 2)
    big = 8 * ROWS * 2
    lo, hi = pl.ds(0, 256), pl.ds(256, 256)
    make(t, "ra", ["mo"], qb.at[:, far, :, :, lo], t1, "y+", big * 256)
    make(t, "rb", ["mo"], qb.at[:, far, :, :, hi], t2, "y-", big * 256)

    def acc(at, c, t_):
        def run():
            qb[:, at, :, :, c] = (qf[:, at, :, :, c] + t_[...].astype(F32)).astype(BF)
        return run
    t.add("raa", ["ra"], acc(right, lo, t1), "compute", cost=0.5)
    make(t, "rc", ["raa"], qb.at[:, right], u1, "y+", big * 512)
    t.add("rbb", ["rb"], acc(left, hi, t2), "compute", cost=0.5)
    make(t, "rd", ["rbb"], qb.at[:, left], u2, "y-", big * 512)

    def sum1():
        r1[...] = qf[:, y] + u1[...].astype(F32) + u2[...].astype(F32)
    t.add("rs", ["rc", "rd"], sum1, "compute", cost=0.8)
    make(t, "rz", ["rs"], r1.at[1 - z], z1, "zA", 128 * 512 * 4)

    def sum2():
        ro[z, y, x] = (r1[z] + z1[...]).astype(BF).reshape(128, 512)
    t.add("rt", ["rz"], sum2, "compute", cost=0.4)
    for p, (row, rows, col, width, order) in enumerate(OUT_GATHER):
        deps = gather("o%d" % p, ro, 2, rows, col, width, order, ["rt"], pl.ds(row, rows))
        t.add("v%d" % p, deps, lambda p=p: write("ro", p), "compute", cost=0.1)

    begun = set()
    for h in range(2):
        ab = abuf.at[h]
        col, muls = 0, []
        for j, (tiles, order) in enumerate(PIECES[h]):
            width = tiles * T
            tag = "a%d%d" % (h, j)
            deps = gather(tag, ab, 2, HALF, col, width, order, ["ld_a"])

            def mul(col=col, width=width, h=h):
                loaded("b")
                first = h not in begun
                begun.add(h)

                def step(s, carry):
                    v = jnp.dot(
                        abuf[h, s, :, :, :, pl.ds(col, width)].reshape(256, width),
                        bvm[pl.ds(col, width), :],
                        preferred_element_type=F32,
                    ).reshape(16, 16, 896)
                    if first:
                        part[h, s] = v
                    else:
                        part[h, s] += v
                    return carry
                lax.fori_loop(0, 2, step, 0)
            t.add(tag + "mul", deps, mul, "compute", cost=tiles * 0.17)
            muls.append(tag + "mul")
            col += width
        k = "e%d" % h
        wide_, thin = 8 * 16 * 896 * 4, 8 * 16 * 896 * 2

        e1, eb, er = ex[h]
        make(t, k + "x", muls, part.at[h, 1 - core], e1, "core", 2 * wide_)

        def add1(h=h, e1=e1, eb=eb):
            v = part[h, core] + e1[...]
            part[h, core] = v
            eb[...] = v.astype(BF)
        t.add(k + "s", [k + "x"], add1, "compute", cost=0.5)
        done = []
        for i in range(2):
            c, rows = k + str(i), pl.ds(i * 8, 8)
            make(t, c + "a", [k + "s"], eb.at[rows], er.at[rows], "z2", thin)

            def add2(h=h, er=er, rows=rows):
                ri[h, core, rows] = (part[h, core, rows] + er[rows].astype(F32)).astype(BF)
            t.add(c + "t", [c + "a"], add2, "compute", cost=0.2)
            mine = ri.at[h, core, rows]
            make(t, c + "f", [c + "t"], mine, mine, "core", thin)
            done += [c + "t", c + "f"]
        t.add("w%d" % h, done, lambda h=h: write("ri", h), "compute", cost=0.1)
    return


def rotate_kernel(acts, grads, bin_, bout, ri_out, ro_out, *scratch):
    (abuf, bvm, part, ro, ri), rest = scratch[:5], scratch[5:]
    rs = rest[0:12]
    ex = [rest[12:15], rest[15:18]]
    ssem, rsem, lsem = rest[18:]
    bo4, g4 = rs[0], rs[3]
    w, n = lax.axis_index("wide"), lax.axis_index("narrow")
    z, y, x = w // 16, (w // 4) % 4, w % 4
    zh, core = n // 2, n % 2
    where = dict(x=x, y=y, z=z, zh=zh, core=core)

    def dev(z_, y_, x_, zh_, core_):
        return {"wide": z_ * 16 + y_ * 4 + x_, "narrow": zh_ * 2 + core_}

    ring = lambda v, d: lax.rem(v + (RING + d), RING)
    peers = {
        "x+": dev(z, y, ring(x, 1), zh, core),
        "x-": dev(z, y, ring(x, -1), zh, core),
        "y+": dev(z, ring(y, 1), x, zh, core),
        "y-": dev(z, ring(y, -1), x, zh, core),
        "zA": dev(1 - z, y, x, zh, core),
        "z2": dev(z, y, x, 1 - zh, core),
        "core": dev(z, y, x, zh, 1 - core),
    }

    local = {}

    def load(name, src, dst):
        c = pltpu.make_async_copy(src, dst, lsem.at[len(local)])
        c.start()
        local[name] = c

    for h in range(2):
        load("a%d" % h, acts.at[pl.ds(h * HALF, HALF)], abuf.at[h, z, y, x])
    load("g", grads, g4.at[x, zh, core])
    load("bo", bout.at[:, pl.ds(pl.multiple_of(x * 512, 512), 512)], bo4.at[x])
    barrier = pltpu.get_barrier_semaphore()
    for p in peers.values():
        pl.semaphore_signal(barrier, inc=1, device_id=p, device_id_type=MESH)
    pl.semaphore_wait(barrier, len(peers))
    load("b", bin_, bvm)

    t = Tasks()
    copies = {}

    def make(t, name, deps, src, dst, link, nbytes):
        i = len(copies)
        copies[name] = (i, src, dst, link)

        def emit():
            d = pltpu.make_async_remote_copy(
                src_ref=src, dst_ref=dst, send_sem=ssem.at[i], recv_sem=rsem.at[i],
                device_id=peers[link], device_id_type=MESH)
            d.start()
            return d
        t.add(name, deps, emit, "send", link, nbytes)

    def loaded(*names):
        for name in names:
            if name in local:
                local.pop(name).wait()

    t.add("ld_a", [], lambda: loaded("a0", "a1"), "compute", cost=0.5)
    t.add("ld_g", [], lambda: loaded("g"), "compute", cost=0.3)

    refs = (bout, abuf, bvm, part, ro, rs, ex, ri)
    outs = []

    def write(what, i):
        if what == "ro":
            row, rows, col, width, _ = OUT_GATHER[i]
            c = (slice(None),) * 3 + (pl.ds(row, rows), pl.ds(col, width))
            pairs = [(ro.at[c], ro_out.at[c])]
        else:
            pairs = [(ri.at[i, s], ri_out.at[s, :, i]) for s in range(SEQS)]
        for src, dst in pairs:
            c = pltpu.make_async_copy(src, dst, lsem.at[4 + len(outs)])
            c.start()
            outs.append(c)

    build(t, refs, where, make, write, loaded)

    started, arrived = {}, set()

    def need(name):
        if name in copies and name not in arrived:
            started[name].wait_recv()
            arrived.add(name)

    names = list(t.items)
    assert sorted(ORDER) == list(range(len(names)))
    for name in [names[i] for i in ORDER]:
        _, deps, emit, kind, _, _ = t.items[name]
        for d in deps:
            need(d)
        r = emit()
        if kind == "send":
            started[name] = r
    for name in copies:
        need(name)
    for name in copies:
        started[name].wait_send()
    for c in outs:
        c.wait()


def rotate(acts, grads, bin_, bout):
    V = pltpu.VMEM
    scratch = [
        V((2, 2, RING, RING, HALF, 7168), BF),
        V((7168, 896), BF),
        V((2, 2, 16, 16, 896), F32),
        V((2, RING, RING, 128, 512), BF),
        V((2, 2, 16, 16, 896), BF),
        V((RING, 256, 512), BF), V((128, 512), BF), V((128, 512), BF),
        V((RING, 2, 2, 256, 256), BF),
        V((2, RING, RING, ROWS, 512), BF),
        V((2, RING, ROWS, 256), BF), V((2, RING, ROWS, 256), BF),
        V((2, RING, ROWS, 512), BF), V((2, RING, ROWS, 512), BF),
        V((2, RING, ROWS, 512), F32), V((RING, ROWS, 512), F32),
        V((2, RING, RING, ROWS, 512), F32),
    ]
    scratch += [V((16, 16, 896), F32), V((16, 16, 896), BF), V((16, 16, 896), BF)] * 2
    count = 240
    scratch += [pltpu.SemaphoreType.DMA((count,)), pltpu.SemaphoreType.DMA((count,)), pltpu.SemaphoreType.DMA((16,))]
    any_ = pl.BlockSpec(memory_space=pl.ANY)
    return pl.pallas_call(
        rotate_kernel,
        out_shape=(
            jax.ShapeDtypeStruct((2, 16, 2, 256 // 16, 896), BF),
            jax.ShapeDtypeStruct((2, RING, RING, 128, 512), BF),
        ),
        in_specs=[any_] * 4,
        out_specs=[any_] * 2,
        scratch_shapes=scratch,
        compiler_params=pltpu.CompilerParams(
            collective_id=0, has_side_effects=True, vmem_limit_bytes=67043328),
        name="rotate",
    )(acts, grads, bin_, bout)


COLS = ((0, 512), (512, 384))


def final_kernel(ro_any, ri_any, o_any, rov, riv, ov, rsem, isem, osem):
    gets, rows = {}, {}
    for m in range(2):
        for s in range(SEQS):
            gets[m, s] = pltpu.make_async_copy(ro_any.at[s, :, pl.ds(2 * m, 2)], rov.at[m, s], rsem.at[m, s])
            gets[m, s].start()
            if m == 0:
                rows[s] = pltpu.make_async_copy(ri_any.at[pl.ds(s * 512, 512)], riv.at[s], isem.at[s])
                rows[s].start()
    puts = []
    for m in range(2):
        for p, (col, width) in enumerate(COLS):
            total = None
            for s in range(SEQS):
                if p == 0:
                    gets[m, s].wait()
                    if m == 0:
                        rows[s].wait()
                g = jnp.concatenate([rov[m, s, :, b].reshape(512, 512) for b in range(2)], axis=1)
                r = lax.dot_general(
                    g, riv[s, :, pl.ds(col, width)], (((0,), (0,)), ((), ())), preferred_element_type=F32)
                total = r * r if total is None else total + r * r
            ov[m, :, pl.ds(col, width)] = total * (1.0 / SEQS)
            part = pltpu.make_async_copy(
                ov.at[m, :, pl.ds(col, width)], o_any.at[pl.ds(m * 1024, 1024), pl.ds(col, width)], osem.at[m, p])
            part.start()
            puts.append(part)
    for part in puts:
        part.wait()


def final(ro, ri):
    any_ = pl.BlockSpec(memory_space=pl.ANY)
    return pl.pallas_call(
        final_kernel,
        in_specs=[any_, any_],
        out_specs=any_,
        out_shape=jax.ShapeDtypeStruct((2048, 896), F32),
        scratch_shapes=[
            pltpu.VMEM((2, SEQS, RING, 2, 128, 512), BF),
            pltpu.VMEM((SEQS, 512, 896), BF),
            pltpu.VMEM((2, 1024, 896), F32),
            pltpu.SemaphoreType.DMA((2, SEQS)),
            pltpu.SemaphoreType.DMA((SEQS,)),
            pltpu.SemaphoreType.DMA((2, 2)),
        ],
        name="final",
    )(ro, ri)


def body(activations, out_grads, basis_in, basis_out):
    ri, ro = rotate(activations, out_grads, basis_in, basis_out)
    return final(ro, ri.reshape(1024, 896))


def solution(mesh):
    in_specs = (P("wide", "narrow"), P("narrow", "wide"), P("narrow", "wide"), P("wide", "narrow"))
    return jax.shard_map(body, mesh=mesh, in_specs=in_specs, out_specs=P("narrow", "wide"), check_vma=False)
```
